32 devices in a mesh: dp: 4 (over y, x), expert: 8 (over z, core).
Axes of the slice: x: 2, y: 2, z: 4, core: 2. Of those that a mesh axis runs over, the one named last changes fastest.
Arguments:
- tokens: bfloat16 [1024, 2048], P(('dp', 'expert')), may hold values from -6 to 6
- grad_out: bfloat16 [1024, 2048], P(('dp', 'expert')), may hold values from -0.59765625 to 0.59765625
- routing: int32 [1024, 8], P(('dp', 'expert')), may hold values from 0 to 15, as said below
- replica: int32 [1024, 8], P(('dp', 'expert')), may hold values from 0 to 1, as said below
- gates: bfloat16 [1024, 8], P(('dp', 'expert')), may hold values from 0.25 to 4
- host_expert: int32 [8], replicated, may hold values from 0 to 15, as said below
- w_gate_up: bfloat16 [16, 2, 768, 2048], P('expert', None, 'dp'), may hold values from -0.125 to 0.125
- w_down: bfloat16 [16, 768, 2048], P('expert', 'dp'), may hold values from -0.21875 to 0.21875
Outputs:
- grad_tokens: bfloat16 [1024, 2048], P(('dp', 'expert'))
- grad_gates: float32 [1024, 8], P(('dp', 'expert'))
- grad_w_gate_up: bfloat16 [16, 2, 768, 2048], P('expert', None, 'dp')
- grad_w_down: bfloat16 [16, 768, 2048], P('expert', 'dp')
The draws below stay inside these ranges and needn't reach their ends.
Inputs may be any that keep to these rules, and one draw needn't show every extreme that they name: `routing`: column k of a token names an expert of 2 * k to 2 * k + 1. Within the rows of one device, experts 2 i and 2 i + 1 are named together exactly 2 * 16 times. `replica`: within the rows of one device, each expert has at most 16 choices marked 0 and at most 16 marked 1; some expert reaches 16 marked 0 from every device, and in every index of dp some expert reaches 16 marked 1 from every device. Only experts listed in host_expert have choices marked 1. `host_expert`: for every device d of the expert axis exactly one of its experts 2 d and 2 d + 1 is listed, and it is listed once.
All inputs are finite; a program needn't handle non-finite values.
Results may differ from the reference program's by a relative error of at most 0.013.
Values may be sent and summed in bfloat16 or wider, within the bound.
A program may use at most 128 MiB of HBM per device.

```python
import jax
import jax.numpy as jnp
from jax import lax

D = 2048
FF = 768
TOPK = 8
TOK_DEV = 32
EXPERTS = 16
TOKENS = 1024
BAND = 2
SLOT = 16
BLOCK = 128
N_DP = 4
N_EXPERT = 8


def routing_layout(key):
    root_key = jax.random.fold_in(key, 4242)
    subkeys = jax.random.split(root_key, 5)
    pairs_all = N_EXPERT
    plus_bit = jax.random.randint(subkeys[0], (pairs_all,), 0, 2).astype(jnp.int32)
    extra_share = jax.random.randint(subkeys[1], (N_DP, N_EXPERT, pairs_all), 0, SLOT + 1).astype(jnp.int32)
    full_pair = jax.random.randint(subkeys[2], (N_DP, 1, 1), 0, pairs_all).astype(jnp.int32)
    pair_iota = lax.broadcasted_iota(jnp.int32, (N_DP, N_EXPERT, pairs_all), 2)
    extra_share = jnp.where(pair_iota == full_pair, SLOT, extra_share)
    layout_shape = (N_DP, N_EXPERT, TOPK, TOK_DEV)
    position = lax.broadcasted_iota(jnp.int32, layout_shape, 3)
    column = lax.broadcasted_iota(jnp.int32, layout_shape, 2)
    pair_ids = column * (BAND // 2) + position // (2 * SLOT)
    within = position % (2 * SLOT)
    extra_rows = jnp.take_along_axis(extra_share, pair_ids.reshape(N_DP, N_EXPERT, TOPK * TOK_DEV), axis=2).reshape(layout_shape)
    plus_side = within < SLOT + extra_rows
    chosen_bit = jnp.take(plus_bit, pair_ids)
    expert = 2 * pair_ids + jnp.where(plus_side, chosen_bit, 1 - chosen_bit)
    copy_flag = ((within >= SLOT) & plus_side).astype(jnp.int32)
    scores = jax.random.randint(subkeys[3], layout_shape, 0, 1048576).astype(jnp.int32) * TOK_DEV + position
    ordering = jnp.argsort(scores, axis=3, stable=True).astype(jnp.int32)
    expert = jnp.take_along_axis(expert, ordering, axis=3)
    copy_flag = jnp.take_along_axis(copy_flag, ordering, axis=3)
    routing = jnp.transpose(expert, (0, 1, 3, 2)).reshape(N_DP * N_EXPERT * TOK_DEV, TOPK).astype(jnp.int32)
    replica = jnp.transpose(copy_flag, (0, 1, 3, 2)).reshape(N_DP * N_EXPERT * TOK_DEV, TOPK).astype(jnp.int32)
    owners = jax.random.permutation(subkeys[4], N_EXPERT).astype(jnp.int32)
    host_list = (2 * owners + jnp.take(plus_bit, owners)).astype(jnp.int32)
    return (routing, replica, host_list)


def draw_routing(key, part):
    return routing_layout(key)[0]


def draw_replica(key, part):
    return routing_layout(key)[1]


def draw_host_expert(key, part):
    return routing_layout(key)[2]


def level_of(key, shape, cuts, low, top_value):
    loudness = 1.0
    for axis_at, shards_of in cuts:
        heights = jax.random.uniform(jax.random.fold_in(jax.random.fold_in(key, 6), axis_at), (shards_of,), jnp.float32, low / len(cuts), top_value / len(cuts))
        loudness = loudness * jnp.repeat(jnp.exp(heights), shape[axis_at] // shards_of).reshape((-1,) + (1,) * (len(shape) - 1 - axis_at))
    return loudness


def gaussian(stream_key, shape, deviation, most, pieces=(), kind=jnp.bfloat16):
    drawn = jax.random.normal(stream_key, shape, jnp.float32) * deviation
    if len(pieces) > 0:
        drawn = level_of(stream_key, shape, pieces, -0.22, 0.18) * drawn
    return jnp.clip(drawn, min=-most, max=most).astype(kind)


def setup_inputs(seed: int = 0) -> dict:
    key_list = jax.random.split(jax.random.key(seed), 9)
    return {
        "tokens": gaussian(key_list[0], (TOKENS, D), 1.0, 6.0, ((0, 32),)),
        "grad_out": gaussian(key_list[1], (TOKENS, D), 0.1, 0.59765625, ((0, 32),)),
        "routing": draw_routing(jax.random.fold_in(key_list[8], 71), 0),
        "replica": draw_replica(jax.random.fold_in(key_list[8], 71), 0),
        "gates": jnp.clip(0.25 + 3.75 * jax.random.uniform(key_list[4], (TOKENS, TOPK), jnp.float32) ** level_of(key_list[4], (TOKENS, TOPK), ((0, 32),), -0.2, 0.2), 0.25, 4.0).astype(jnp.bfloat16),
        "host_expert": draw_host_expert(jax.random.fold_in(key_list[8], 71), 0),
        "w_gate_up": gaussian(key_list[6], (EXPERTS, 2, FF, D), D ** -0.5, 0.125, ((0, 8), (2, 4))),
        "w_down": gaussian(key_list[7], (EXPERTS, FF, D), FF ** -0.5, 0.21875, ((0, 8), (1, 4))),
    }


def expert_pass(tokens, grad_out, gates, row_ids, live_rows, gate_up_w, down_w):
    token_ids = row_ids // TOPK
    live_mask = live_rows.astype(tokens.dtype)
    inputs = tokens[token_ids] * live_mask[:, None]
    upstream = grad_out[token_ids] * live_mask[:, None]
    weight = gates.reshape(-1)[row_ids] * live_mask
    quarter = FF // N_DP
    gate_up = gate_up_w.astype(jnp.float32).reshape(2, N_DP, quarter, D)
    down_matrix = down_w.astype(jnp.float32).reshape(N_DP, quarter, D)
    highest = lax.Precision.HIGHEST
    mixed_pre = jnp.einsum("rd,jqfd->rjqf", inputs.astype(jnp.float32), gate_up, precision=highest)
    gate_pre = mixed_pre[:, 0]
    up_part = mixed_pre[:, 1]
    sigmoid_gate = jax.nn.sigmoid(gate_pre)
    active = gate_pre * sigmoid_gate
    hidden = (active * up_part).astype(jnp.bfloat16)
    output_part = jnp.einsum("rqf,qfd->qrd", hidden.astype(jnp.float32), down_matrix, precision=highest)
    gate_part = jnp.sum(output_part * upstream.astype(jnp.float32)[None], axis=2).astype(jnp.bfloat16)
    row_dg = jnp.sum(gate_part.astype(jnp.float32), axis=0).astype(jnp.bfloat16)
    scaled = (weight.astype(jnp.float32)[:, None] * upstream.astype(jnp.float32)).astype(jnp.bfloat16)
    grad_hidden = jnp.einsum("rd,qfd->rqf", scaled.astype(jnp.float32), down_matrix, precision=highest)
    grad_gate = grad_hidden * up_part * sigmoid_gate * (1.0 + gate_pre * (1.0 - sigmoid_gate))
    grad_mixed = jnp.stack([grad_gate, grad_hidden * active], axis=1).astype(jnp.bfloat16)
    input_part = jnp.einsum("rjqf,jqfd->qrd", grad_mixed.astype(jnp.float32), gate_up, precision=highest)
    row_dx = jnp.sum(input_part.astype(jnp.bfloat16).astype(jnp.float32), axis=0).astype(jnp.bfloat16)
    weight_gu = jnp.einsum("rd,rjqf->jqfd", inputs.astype(jnp.float32), grad_mixed.astype(jnp.float32), precision=highest)
    weight_down = jnp.einsum("rqf,rd->qfd", hidden.astype(jnp.float32), scaled.astype(jnp.float32), precision=highest)
    return row_dx, row_dg, weight_gu.reshape(2, FF, D), weight_down.reshape(FF, D)


def reference(tokens, grad_out, routing, replica, gates, host_expert, w_gate_up, w_down):
    expert_ids = lax.broadcasted_iota(jnp.int32, (EXPERTS, N_EXPERT), 0)
    helper_ids = lax.broadcasted_iota(jnp.int32, (EXPERTS, N_EXPERT), 1)
    matches = host_expert[None, :] == expert_ids
    listed = jnp.sum(matches.astype(jnp.int32), axis=1)
    helper_of = jnp.sum(jnp.where(matches, helper_ids, 0), axis=1).astype(jnp.int32)
    flat_route = routing.reshape(-1).astype(jnp.int32)
    flat_copy = replica.reshape(-1).astype(jnp.int32)
    usable = (flat_copy == 0) | (listed[flat_route] > 0)
    labels = jnp.where(usable, flat_copy * EXPERTS + flat_route, 2 * EXPERTS).astype(jnp.int32)
    ordering = jnp.argsort(labels, stable=True).astype(jnp.int32)
    counts = jnp.bincount(labels, length=2 * EXPERTS + 1).astype(jnp.int32)
    starts = (jnp.cumsum(counts) - counts).astype(jnp.int32)
    capacity = N_DP * BLOCK
    padded = jnp.concatenate([ordering, jnp.zeros((capacity,), jnp.int32)])

    def segment(label_id):
        row_ids = lax.dynamic_slice_in_dim(padded, starts[label_id], capacity).astype(jnp.int32)
        live_rows = lax.broadcasted_iota(jnp.int32, (capacity,), 0) < counts[label_id]
        return row_ids, live_rows

    def accumulate(totals, row_ids, live_rows, row_dx, row_dg):
        grad_tok, grad_row = totals
        live_mask = live_rows.astype(jnp.float32)
        grad_tok = grad_tok.at[row_ids // TOPK].add(row_dx.astype(jnp.float32) * live_mask[:, None])
        grad_row = grad_row.at[row_ids].add(row_dg.astype(jnp.float32) * live_mask)
        return grad_tok, grad_row

    def helper_step(totals, expert):
        row_ids, live_rows = segment(EXPERTS + expert)
        row_dx, row_dg, weight_gu, weight_down = expert_pass(tokens, grad_out, gates, row_ids, live_rows, w_gate_up[expert], w_down[expert])
        totals = accumulate(totals, row_ids, live_rows, row_dx, row_dg)
        return totals, (weight_gu.astype(jnp.bfloat16), weight_down.astype(jnp.bfloat16))

    start_totals = (jnp.zeros((TOKENS, D), jnp.float32), jnp.zeros((TOKENS * TOPK,), jnp.float32))
    totals, helper_parts = lax.scan(helper_step, start_totals, host_expert.astype(jnp.int32))
    helper_gu, helper_down = helper_parts

    def owner_step(totals, expert):
        row_ids, live_rows = segment(expert)
        row_dx, row_dg, weight_gu, weight_down = expert_pass(tokens, grad_out, gates, row_ids, live_rows, w_gate_up[expert], w_down[expert])
        totals = accumulate(totals, row_ids, live_rows, row_dx, row_dg)
        present = (listed[expert] > 0).astype(jnp.float32)
        extra_gu = helper_gu[helper_of[expert]].astype(jnp.float32) * present
        extra_down = helper_down[helper_of[expert]].astype(jnp.float32) * present
        return totals, ((weight_gu + extra_gu).astype(jnp.bfloat16), (weight_down + extra_down).astype(jnp.bfloat16))

    totals, owner_parts = lax.scan(owner_step, totals, jnp.arange(EXPERTS, dtype=jnp.int32))
    grad_tok, grad_row = totals
    grad_w_gate_up, grad_w_down = owner_parts
    return grad_tok.astype(jnp.bfloat16), grad_row.reshape(TOKENS, TOPK), grad_w_gate_up, grad_w_down
```

```python
import functools

import jax
import jax.numpy as jnp
from jax import lax
from jax.experimental import pallas as pl
from jax.experimental.pallas import tpu as pltpu
from jax.sharding import PartitionSpec as P

MESH = pl.DeviceIdType.MESH


def lookup(values_table, indices):
    matches = indices[..., None] == lax.broadcasted_iota(
        jnp.int32, indices.shape + values_table.shape, indices.ndim
    )
    return jnp.sum(jnp.where(matches, values_table, 0), axis=-1)


def placement(host_expert, owned_experts, devices):
    experts = owned_experts * devices
    matches = host_expert[None, :] == lax.broadcasted_iota(jnp.int32, (experts, devices), 0)
    helper_ids = lax.broadcasted_iota(jnp.int32, (experts, devices), 1)
    helper_of = jnp.sum(jnp.where(matches, helper_ids, 0), axis=1)
    listed = jnp.sum(matches.astype(jnp.int32), axis=1)
    return (helper_of, listed)


def targets(routing, replica, host_expert, owned_experts, devices, slot_rows, groups):
    helper_of, listed = placement(host_expert, owned_experts, devices)
    choices = routing.shape[0] // groups * routing.shape[1]
    usable = (replica == 0) | (lookup(listed, routing) > 0)
    device_to = jnp.where(replica == 0, routing // owned_experts, lookup(helper_of, routing))
    block_to = jnp.where(replica == 0, routing % owned_experts, owned_experts)
    labels = (routing * 2 + replica).reshape(groups, choices)
    earlier = lax.broadcasted_iota(jnp.int32, (choices, choices), 1) < lax.broadcasted_iota(
        jnp.int32, (choices, choices), 0
    )
    matching = (labels[:, :, None] == labels[:, None, :]) & earlier[None]
    ranking = jnp.sum(matching.astype(jnp.int32), axis=2).reshape(routing.shape)
    group_ids = lax.broadcasted_iota(jnp.int32, (groups, choices), 0).reshape(routing.shape)
    position = ((block_to * groups + group_ids) * devices + device_to) * slot_rows + ranking
    return jnp.where(usable, position, -1)


def selector(position, total_slots):
    matches = position[None, :, :] == lax.broadcasted_iota(
        jnp.int32, (total_slots,) + position.shape, 0
    )
    picker = jnp.sum(matches.astype(jnp.float32), axis=2).astype(jnp.bfloat16)
    return (matches, picker)


def fill_rows(matches, picker, tokens, grad_out, gates):
    row_x = jnp.dot(picker, tokens, preferred_element_type=jnp.float32).astype(jnp.bfloat16)
    row_dy = jnp.dot(picker, grad_out, preferred_element_type=jnp.float32).astype(jnp.bfloat16)
    row_gate = jnp.sum(
        jnp.where(matches, gates[None].astype(jnp.float32), 0.0), axis=(1, 2)
    ).astype(jnp.bfloat16)
    return (row_x, row_dy, row_gate)


def expert_block(inputs, upstream, weight, gate_up, down_matrix):
    mixed = jnp.einsum("rd,jfd->jrf", inputs, gate_up, preferred_element_type=jnp.float32)
    gate_pre = mixed[0]
    up_part = mixed[1]
    sigmoid_gate = jax.nn.sigmoid(gate_pre)
    active = gate_pre * sigmoid_gate
    hidden = (active * up_part).astype(jnp.bfloat16)
    output_part = jnp.einsum("rf,fd->rd", hidden, down_matrix, preferred_element_type=jnp.float32)
    gate_part = jnp.sum(output_part * upstream.astype(jnp.float32), axis=1)
    scaled = (weight.astype(jnp.float32)[:, None] * upstream.astype(jnp.float32)).astype(
        jnp.bfloat16
    )
    grad_hidden = jnp.einsum("rd,fd->rf", scaled, down_matrix, preferred_element_type=jnp.float32)
    grad_gate = grad_hidden * up_part * sigmoid_gate * (1.0 + gate_pre * (1.0 - sigmoid_gate))
    grad_mixed = jnp.stack([grad_gate, grad_hidden * active], axis=0).astype(jnp.bfloat16)
    input_part = jnp.einsum("jrf,jfd->rd", grad_mixed, gate_up, preferred_element_type=jnp.float32)
    weight_gu = jnp.einsum("jrf,rd->jfd", grad_mixed, inputs, preferred_element_type=jnp.float32)
    weight_down = jnp.einsum("rf,rd->fd", hidden, scaled, preferred_element_type=jnp.float32)
    return (input_part, gate_part, weight_gu, weight_down)


def shards(tokens, grad_out, routing, replica, gates, host_expert, w_gate_up, w_down):
    devices = lax.axis_size("expert")
    device_id = lax.axis_index("expert")
    token_rows, features = tokens.shape
    owned_experts = w_gate_up.shape[0]
    quarter = w_down.shape[1]
    topk_width = routing.shape[1]
    slot_rows = token_rows * topk_width // (owned_experts * devices)
    blocks = owned_experts + 1
    lane_rows = devices * slot_rows
    piece_rows = quarter // devices
    home_slots = targets(routing, replica, host_expert, owned_experts, devices, slot_rows, 1)
    home_matches, home_picker = selector(home_slots, blocks * lane_rows)
    row_x, row_dy, row_gate = fill_rows(home_matches, home_picker, tokens, grad_out, gates)
    sent_x, sent_dy, sent_gate = (
        lax.all_to_all(
            row_x.reshape(blocks, lane_rows, features),
            "expert",
            split_axis=1,
            concat_axis=1,
            tiled=True,
        ),
        lax.all_to_all(
            row_dy.reshape(blocks, lane_rows, features),
            "expert",
            split_axis=1,
            concat_axis=1,
            tiled=True,
        ),
        lax.all_to_all(
            row_gate.reshape(blocks, lane_rows), "expert", split_axis=1, concat_axis=1, tiled=True
        ),
    )
    block_x, block_dy, block_gate = (
        lax.all_gather(sent_x, "dp", axis=1, tiled=True),
        lax.all_gather(sent_dy, "dp", axis=1, tiled=True),
        lax.all_gather(sent_gate, "dp", axis=1, tiled=True),
    )
    owner_of_helper = host_expert // owned_experts
    owns_copy = owner_of_helper == device_id
    copied_local = jnp.sum(jnp.where(owns_copy, host_expert % owned_experts, 0))
    helper_ids = lax.broadcasted_iota(jnp.int32, (devices, devices), 1)
    owner_ids = lax.broadcasted_iota(jnp.int32, (devices, devices), 0)
    helper_of_owner = jnp.sum(
        jnp.where(owner_of_helper[None, :] == owner_ids, helper_ids, 0), axis=1
    )
    source_gu = lax.dynamic_index_in_dim(w_gate_up, copied_local, 0, keepdims=False)
    source_down = lax.dynamic_index_in_dim(w_down, copied_local, 0, keepdims=False)
    spread_gu, spread_down = (
        lax.all_to_all(
            source_gu.reshape(2, devices, piece_rows, features),
            "expert",
            split_axis=1,
            concat_axis=1,
            tiled=True,
        ),
        lax.all_to_all(
            source_down.reshape(1, devices, piece_rows, features),
            "expert",
            split_axis=1,
            concat_axis=1,
            tiled=True,
        ),
    )
    spread_gu = jnp.take(spread_gu, owner_of_helper, axis=1)
    spread_down = jnp.take(spread_down, owner_of_helper, axis=1)
    hosted_gu, hosted_down = (
        lax.all_to_all(spread_gu, "expert", split_axis=1, concat_axis=1, tiled=True),
        lax.all_to_all(spread_down, "expert", split_axis=1, concat_axis=1, tiled=True),
    )
    hosted_gu = hosted_gu.reshape(2, quarter, features)
    hosted_down = hosted_down.reshape(quarter, features)
    input_parts = []
    gate_parts = []
    owner_gu = []
    owner_down = []
    for block in range(blocks):
        if block < owned_experts:
            gate_up = w_gate_up[block]
            down_matrix = w_down[block]
        else:
            gate_up = hosted_gu
            down_matrix = hosted_down
        input_part, gate_part, weight_gu, weight_down = expert_block(
            block_x[block], block_dy[block], block_gate[block], gate_up, down_matrix
        )
        input_parts.append(input_part.astype(jnp.bfloat16))
        gate_parts.append(gate_part.astype(jnp.bfloat16))
        owner_gu.append(weight_gu)
        owner_down.append(weight_down)
    helper_gu = owner_gu[owned_experts].astype(jnp.bfloat16)
    helper_down = owner_down[owned_experts].astype(jnp.bfloat16)
    back_gu, back_down = (
        lax.all_to_all(
            helper_gu.reshape(2, devices, piece_rows, features),
            "expert",
            split_axis=1,
            concat_axis=1,
            tiled=True,
        ),
        lax.all_to_all(
            helper_down.reshape(1, devices, piece_rows, features),
            "expert",
            split_axis=1,
            concat_axis=1,
            tiled=True,
        ),
    )
    back_gu = jnp.take(back_gu, helper_of_owner, axis=1)
    back_down = jnp.take(back_down, helper_of_owner, axis=1)
    extra_gu, extra_down = (
        lax.all_to_all(back_gu, "expert", split_axis=1, concat_axis=1, tiled=True),
        lax.all_to_all(back_down, "expert", split_axis=1, concat_axis=1, tiled=True),
    )
    extra_gu = extra_gu.reshape(2, quarter, features).astype(jnp.float32)
    extra_down = extra_down.reshape(quarter, features).astype(jnp.float32)
    stacked_dx = jnp.stack(input_parts, axis=0)
    stacked_dg = jnp.stack(gate_parts, axis=0)
    summed_dx, summed_dg = (
        lax.psum_scatter(stacked_dx, "dp", scatter_dimension=1, tiled=True).astype(jnp.float32),
        lax.psum_scatter(stacked_dg, "dp", scatter_dimension=1, tiled=True).astype(jnp.float32),
    )
    row_dx = summed_dx.astype(jnp.bfloat16)
    row_dg = summed_dg.astype(jnp.bfloat16)
    home_dx, home_dg = (
        lax.all_to_all(row_dx, "expert", split_axis=1, concat_axis=1, tiled=True),
        lax.all_to_all(row_dg, "expert", split_axis=1, concat_axis=1, tiled=True),
    )
    home_dx = home_dx.reshape(blocks * lane_rows, features)
    home_dg = home_dg.reshape(blocks * lane_rows).astype(jnp.float32)
    grad_tokens = jnp.einsum(
        "st,sd->td", home_picker, home_dx, preferred_element_type=jnp.float32
    ).astype(jnp.bfloat16)
    grad_gates = jnp.sum(jnp.where(home_matches, home_dg[:, None, None], 0.0), axis=0)
    grad_gu = []
    grad_down = []
    for block in range(owned_experts):
        present = (copied_local == block).astype(jnp.float32)
        grad_gu.append((owner_gu[block] + present * extra_gu).astype(jnp.bfloat16))
        grad_down.append((owner_down[block] + present * extra_down).astype(jnp.bfloat16))
    return (grad_tokens, grad_gates, jnp.stack(grad_gu, axis=0), jnp.stack(grad_down, axis=0))


OWN, ACROSS, ALONG, DIAGONAL = range(4)
PARTNER, TO_X, TO_Y, INNER, OUTER = range(5)
OWN_X, OWN_Y, OWN_INNER, OWN_OUTER, ACROSS_Y, ALONG_X, DIAGONAL_INNER, DIAGONAL_OUTER = range(8)
ALL, END, MID = range(3)


def usable_choices(routing, replica, host_ref):
    usable = replica == 0
    for index in range(host_ref.shape[0]):
        usable = usable | (routing == host_ref[index])
    return usable


def fused_kernel(
    experts,
    tokens_hbm,
    grad_out_hbm,
    routing_hbm,
    replica_hbm,
    gates_hbm,
    host_hbm,
    gu_hbm,
    down_hbm,
    tokens_out,
    gates_out,
    grad_gu_ref,
    grad_down_ref,
    rows_ref,
    gu_ref,
    down_ref,
    mixed_ref,
    hidden_ref,
    part_ref,
    paired_ref,
    inbox_ref,
    routing_ref,
    replica_ref,
    gates_ref,
    host_ref,
    local,
    sent,
    landed,
    pair_sent,
    pair_landed,
    sums_sent,
    sums_landed,
):
    dp = lax.axis_index("dp")
    expert = lax.axis_index("expert")
    height, core = expert // 2, expert % 2
    row, column = dp // 2, dp % 2
    depth = rows_ref.shape[0] // 4
    count = rows_ref.shape[2]
    half = count // 2
    features = tokens_hbm.shape[1]
    lanes = rows_ref.shape[3] - 2 * features
    owned, quarter = down_ref.shape[:2]
    across = row * 2 + 1 - column
    along = (1 - row) * 2 + column
    roles = (dp, across, along, (1 - row) * 2 + 1 - column)
    upper = height // (depth // 2)
    levels = (
        height,
        height + 1 - 2 * (height % 2),
        depth // 2 - upper,
        (depth - 1) * (1 - upper),
    )
    is_mid = (height + upper) % 2 == 1
    is_end = (height + upper) % 2 == 0
    inner_level = height + 1 - 2 * upper
    targets_of = (
        (dp, height * 2 + 1 - core),
        (across, expert),
        (along, expert),
        (dp, inner_level * 2 + core),
        (dp, levels[1] * 2 + core),
    )
    scope = [ALL]
    unsent = ([], [], [])

    def within(role, body):
        scope[0] = role

        @pl.when(is_end if role == END else is_mid)
        def _():
            body()

        scope[0] = ALL

    def begin(make, *args):
        make(*args).start()
        unsent[scope[0]].append((make, args))

    def chip(role, near):
        return roles[role] * depth + levels[near]

    mine = chip(OWN, 0)
    loads = [
        pltpu.make_async_copy(routing_hbm, routing_ref, local.at[0]),
        pltpu.make_async_copy(replica_hbm, replica_ref, local.at[1]),
        pltpu.make_async_copy(gates_hbm, gates_ref, local.at[2]),
        pltpu.make_async_copy(host_hbm, host_ref, local.at[3]),
        pltpu.make_async_copy(tokens_hbm, rows_ref.at[mine, core, :, pl.ds(0, features)], local.at[4]),
        pltpu.make_async_copy(
            grad_out_hbm, rows_ref.at[mine, core, :, pl.ds(features, features)], local.at[5]
        ),
        pltpu.make_async_copy(gu_hbm, gu_ref, local.at[6]),
        pltpu.make_async_copy(down_hbm, down_ref, local.at[7]),
    ]
    for load in loads:
        load.start()
    barrier = pltpu.get_barrier_semaphore()
    for way in (PARTNER, TO_X, TO_Y, INNER):
        pl.semaphore_signal(barrier, inc=1, device_id=targets_of[way], device_id_type=MESH)

    @pl.when(is_mid)
    def _():
        pl.semaphore_signal(barrier, inc=1, device_id=targets_of[OUTER], device_id_type=MESH)

    for load in loads[:4]:
        load.wait()
    routing = routing_ref[...]
    usable = usable_choices(routing, replica_ref[...], host_ref)
    gates = jnp.where(usable, gates_ref[...].astype(jnp.float32), 0.0)
    weights = jnp.concatenate(
        [
            jnp.sum(jnp.where(routing == index, gates, 0.0), axis=0, keepdims=True)
            for index in range(experts)
        ]
        + [jnp.zeros((lanes - experts, count), jnp.float32)],
        axis=0,
    )
    rows_ref[mine, core, :, 2 * features :] = weights.T.astype(jnp.bfloat16)
    for load in loads[4:6]:
        load.wait()
    pl.semaphore_wait(barrier, 4 + is_mid.astype(jnp.int32))

    def piece(part):
        return pl.ds(part * half, half)

    def row_copy(role, near, part, way):
        at = chip(role, near)
        block = rows_ref.at[at, core] if part is None else rows_ref.at[at, core, piece(part)]
        index = 0 if part is None else part
        return pltpu.make_async_remote_copy(
            src_ref=block,
            dst_ref=block,
            send_sem=sent.at[at, way * 2 + index],
            recv_sem=landed.at[at, core, index],
            device_id=targets_of[way],
            device_id_type=MESH,
        )

    def forward(role, near, part, *ways):
        for way in ways:
            begin(row_copy, role, near, part, way)

    def arrive(role, near, part):
        row_copy(role, near, part, PARTNER).wait_recv()

    def relay(role, near, part, *ways):
        arrive(role, near, part)
        forward(role, near, part, *ways)
        if part == 1:
            forward(role, near, None, PARTNER)

    def partner_rows(role, near):
        at = chip(role, near)
        block = rows_ref.at[at, 1 - core]
        pltpu.make_async_remote_copy(
            src_ref=block,
            dst_ref=block,
            send_sem=sent.at[at, 0],
            recv_sem=landed.at[at, 1 - core, 0],
            device_id=targets_of[PARTNER],
            device_id_type=MESH,
        ).wait_recv()

    def rows_by_columns(a, b):
        return lax.dot_general(
            a, b, (((1,), (1,)), ((), ())), preferred_element_type=jnp.float32
        )

    def columns_by_columns(a, b):
        return lax.dot_general(
            a, b, (((0,), (0,)), ((), ())), preferred_element_type=jnp.float32
        ).astype(jnp.bfloat16)

    chip_rows = 2 * count

    def pair_copy(at):
        return pltpu.make_async_remote_copy(
            src_ref=part_ref.at[at, 1 - core],
            dst_ref=paired_ref.at[at],
            send_sem=pair_sent.at[at],
            recv_sem=pair_landed.at[at],
            device_id=targets_of[PARTNER],
            device_id_type=MESH,
        )

    def compute(*group):
        chips = [chip(role, near) for role, near in group]
        for role, near in group:
            partner_rows(role, near)

        def take(first, size):
            return jnp.concatenate(
                [
                    rows_ref[at, :, :, first : first + size].reshape(chip_rows, size)
                    for at in chips
                ],
                axis=0,
            )

        inputs = take(0, features)
        upstream = take(features, features)
        side = take(2 * features, lanes).astype(jnp.float32)
        slots = lax.broadcasted_iota(jnp.int32, side.shape, 1)
        gate_side = jnp.zeros(side.shape, jnp.float32)
        grads = []
        for local_expert in range(owned):
            at_expert = slots == expert * owned + local_expert
            weight = jnp.sum(jnp.where(at_expert, side, 0.0), axis=1, keepdims=True)
            gate_pre = rows_by_columns(inputs, gu_ref[local_expert, 0])
            up_part = rows_by_columns(inputs, gu_ref[local_expert, 1])
            raw_hidden = rows_by_columns(upstream, down_ref[local_expert])
            sigmoid_gate = jax.nn.sigmoid(gate_pre)
            active = gate_pre * sigmoid_gate
            hidden = (active * up_part).astype(jnp.bfloat16).astype(jnp.float32)
            gate_part = jnp.sum(hidden * raw_hidden, axis=1, keepdims=True)
            gate_side = jnp.where(at_expert, gate_part, gate_side)
            grad_hidden = raw_hidden * weight
            grad_gate = (
                grad_hidden * up_part * sigmoid_gate * (1.0 + gate_pre * (1.0 - sigmoid_gate))
            )
            weighted = (hidden * weight).astype(jnp.bfloat16)
            grads.append(grad_gate.astype(jnp.bfloat16))
            grads.append((grad_hidden * active).astype(jnp.bfloat16))
            for index, at in enumerate(chips):
                span = slice(index * chip_rows, (index + 1) * chip_rows)
                hidden_ref[local_expert, at] = weighted[span]
                mixed_ref[2 * local_expert, at] = grads[-2][span]
                mixed_ref[2 * local_expert + 1, at] = grads[-1][span]
        dx = jnp.zeros(inputs.shape, jnp.float32)
        for index in range(2 * owned):
            dx = dx + jnp.dot(
                grads[index],
                gu_ref[index // 2, index % 2],
                preferred_element_type=jnp.float32,
            )
        for index, at in enumerate(chips):
            span = slice(index * chip_rows, (index + 1) * chip_rows)
            part_ref[at, :, :, :features] = (
                dx[span].astype(jnp.bfloat16).reshape(2, count, features)
            )
            part_ref[at, :, :, features:] = (
                gate_side[span].astype(jnp.bfloat16).reshape(2, count, lanes)
            )
            begin(pair_copy, at)

    def combine(*group):
        for role, near in group:
            at = chip(role, near)
            pair_copy(at).wait_recv()
            part_ref[at, core] = (
                part_ref[at, core].astype(jnp.float32) + paired_ref[at].astype(jnp.float32)
            ).astype(jnp.bfloat16)

    def box_index(box, role, near, part):
        return (box * depth + levels[near]) * 2 + part

    def sum_copy(role, near, part, way, box):
        index = box_index(box, role, near, part)
        return pltpu.make_async_remote_copy(
            src_ref=part_ref.at[chip(role, near), core, piece(part)],
            dst_ref=inbox_ref.at[index],
            send_sem=sums_sent.at[index],
            recv_sem=sums_landed.at[index],
            device_id=targets_of[way],
            device_id_type=MESH,
        )

    def incoming(role, near, part, box):
        index = box_index(box, role, near, part)
        sum_copy(role, near, part, PARTNER, box).wait_recv()
        return inbox_ref[index].astype(jnp.float32)

    def send_sum(role, near, part, way):
        if way == TO_X:
            box = ALONG_X if role == DIAGONAL else OWN_X
        elif way == TO_Y:
            box = ACROSS_Y if role == DIAGONAL else OWN_Y
        else:
            outward = way == INNER and scope[0] == END
            box = (OWN_OUTER if outward else OWN_INNER) if role == OWN else (
                DIAGONAL_OUTER if outward else DIAGONAL_INNER
            )
        begin(sum_copy, role, near, part, way, box)

    def gather_sums(role, near, part, way, *boxes):
        at = chip(role, near)
        if boxes:
            value = part_ref[at, core, piece(part)].astype(jnp.float32)
            for box in boxes:
                value = value + incoming(role, near, part, box)
            part_ref[at, core, piece(part)] = value.astype(jnp.bfloat16)
        send_sum(role, near, part, way)

    total_rows = 4 * depth * chip_rows

    def down_grad(local_expert):
        upstream = rows_ref[:, :, :, features : 2 * features].reshape(total_rows, features)
        weighted = hidden_ref[local_expert].reshape(total_rows, quarter)
        grad_down_ref[local_expert] = columns_by_columns(weighted, upstream)

    def gu_grad(index):
        inputs = rows_ref[:, :, :, :features].reshape(total_rows, features)
        grads = mixed_ref[index].reshape(total_rows, quarter)
        grad_gu_ref[index // 2, index % 2] = columns_by_columns(grads, inputs)

    forward(OWN, 0, 0, INNER, TO_X, TO_Y)
    within(MID, lambda: forward(OWN, 0, 0, OUTER))
    forward(OWN, 0, 1, INNER, TO_X, TO_Y)
    within(MID, lambda: forward(OWN, 0, 1, OUTER))
    forward(OWN, 0, None, PARTNER)

    def end_first():
        relay(ACROSS, 0, 0, TO_Y)
        relay(OWN, 1, 0, TO_X, TO_Y)
        relay(ALONG, 0, 0)
        relay(ALONG, 0, 1, TO_X)
        relay(OWN, 1, 1, TO_X, TO_Y)
        relay(ACROSS, 0, 1)

    def mid_first():
        relay(OWN, 1, 0, INNER, TO_X)
        relay(OWN, 2, 0, OUTER)
        relay(ACROSS, 0, 0, TO_Y)
        forward(OWN, 1, 0, TO_Y)
        relay(ALONG, 0, 0)
        relay(OWN, 1, 1, INNER)
        relay(OWN, 2, 1, OUTER)
        relay(ALONG, 0, 1, TO_X)
        forward(OWN, 1, 1, TO_X, TO_Y)
        relay(ACROSS, 0, 1)
        forward(OWN, 2, 0, TO_X, TO_Y)
        forward(OWN, 2, 1, TO_X, TO_Y)

    within(END, end_first)
    within(MID, mid_first)
    for load in loads[6:]:
        load.wait()
    compute((OWN, 0), (OWN, 1))

    def end_second():
        relay(DIAGONAL, 0, 0, INNER)
        relay(OWN, 2, 0, TO_X, TO_Y)
        relay(DIAGONAL, 0, 1, INNER)
        relay(OWN, 2, 1, TO_X, TO_Y)

    def mid_second():
        relay(OWN, 3, 0, OUTER)
        relay(DIAGONAL, 0, 0, INNER)
        relay(OWN, 3, 1, OUTER)
        relay(DIAGONAL, 0, 1, INNER)
        forward(OWN, 3, 0, TO_X, TO_Y)
        forward(OWN, 3, 1, TO_X, TO_Y)

    within(END, end_second)
    within(MID, mid_second)
    compute((ACROSS, 0), (ALONG, 0))

    def end_third():
        relay(ACROSS, 1, 0)
        relay(ALONG, 1, 0)
        relay(OWN, 3, 0, TO_X, TO_Y)

    def mid_third():
        relay(ACROSS, 1, 0)
        relay(ALONG, 1, 0)
        relay(DIAGONAL, 1, 0, INNER)
        relay(DIAGONAL, 2, 0, OUTER)

    within(END, end_third)
    within(MID, mid_third)
    compute((DIAGONAL, 0), (OWN, 2))
    combine((OWN, 0), (OWN, 1))

    def end_fourth():
        relay(ACROSS, 1, 1)
        relay(ALONG, 1, 1)
        relay(OWN, 3, 1, TO_X, TO_Y)
        forward(ACROSS, 1, 0, TO_Y)
        forward(ALONG, 1, 1, TO_X)

    def mid_fourth():
        relay(DIAGONAL, 1, 1, INNER)
        relay(DIAGONAL, 2, 1, OUTER)
        relay(ACROSS, 1, 1)
        relay(ALONG, 1, 1)

    within(END, end_fourth)
    within(MID, mid_fourth)
    compute((ACROSS, 1), (ALONG, 1))
    combine((ACROSS, 0), (ALONG, 0))
    within(MID, lambda: relay(DIAGONAL, 3, 0, OUTER))
    for part in range(2):
        relay(ACROSS, 2, part)
        relay(ALONG, 2, part)
    within(MID, lambda: relay(DIAGONAL, 3, 1, OUTER))
    compute((OWN, 3), (ACROSS, 2))
    combine((DIAGONAL, 0), (OWN, 2))
    within(END, lambda: [relay(DIAGONAL, 2, part) for part in range(2)])
    compute((ALONG, 2), (DIAGONAL, 2))
    combine((ACROSS, 1), (ALONG, 1))
    combine((OWN, 3), (ACROSS, 2))
    for part in range(2):
        relay(ACROSS, 3, part)
        relay(ALONG, 3, part)
    compute((ACROSS, 3), (ALONG, 3))
    combine((ALONG, 2), (DIAGONAL, 2))
    for part in range(2):
        gather_sums(ACROSS, 2, part, TO_X)
        gather_sums(ALONG, 2, part, TO_Y)
        within(END, lambda: gather_sums(DIAGONAL, 2, part, INNER))
    within(
        END,
        lambda: [
            relay(DIAGONAL, near, part) for part in range(2) for near in (1, 3)
        ],
    )
    compute((DIAGONAL, 1), (DIAGONAL, 3))
    combine((ACROSS, 3), (ALONG, 3))
    for part in range(2):
        gather_sums(ACROSS, 3, part, TO_X)
        gather_sums(ALONG, 3, part, TO_Y)
    combine((DIAGONAL, 1), (DIAGONAL, 3))

    def end_fifth():
        for part in range(2):
            gather_sums(DIAGONAL, 3, part, INNER)
        gather_sums(DIAGONAL, 1, 0, TO_Y)
        gather_sums(DIAGONAL, 1, 1, TO_X)

    def mid_fifth():
        for part in range(2):
            gather_sums(DIAGONAL, 2, part, INNER, DIAGONAL_OUTER)

    within(END, end_fifth)
    within(MID, mid_fifth)
    down_grad(0)

    def end_sixth():
        for part in range(2):
            gather_sums(OWN, 2, part, INNER, OWN_X, OWN_Y)

    def mid_sixth():
        for part in range(2):
            gather_sums(DIAGONAL, 3, part, INNER, DIAGONAL_OUTER)
        for part in range(2):
            gather_sums(DIAGONAL, 1, part, OUTER, DIAGONAL_INNER)

    within(END, end_sixth)
    within(MID, mid_sixth)
    down_grad(1)

    def end_seventh():
        for part in range(2):
            gather_sums(OWN, 3, part, INNER, OWN_X, OWN_Y)
        gather_sums(ACROSS, 1, 0, TO_X, ACROSS_Y)
        gather_sums(ACROSS, 1, 1, TO_X)
        gather_sums(ALONG, 1, 0, TO_Y)
        gather_sums(ALONG, 1, 1, TO_Y, ALONG_X)

    def mid_seventh():
        for part in range(2):
            gather_sums(ACROSS, 1, part, TO_X)
            gather_sums(ALONG, 1, part, TO_Y)
        for part in range(2):
            gather_sums(OWN, 2, part, INNER, OWN_X, OWN_Y, OWN_OUTER)

    within(END, end_seventh)
    within(MID, mid_seventh)
    gu_grad(0)

    def diagonal_home():
        gather_sums(DIAGONAL, 0, 0, TO_Y, DIAGONAL_INNER)
        gather_sums(DIAGONAL, 0, 1, TO_X, DIAGONAL_INNER)

    def mid_eighth():
        for part in range(2):
            gather_sums(OWN, 3, part, INNER, OWN_X, OWN_Y, OWN_OUTER)

    within(MID, mid_eighth)
    diagonal_home()
    gu_grad(1)
    for part in range(2):
        within(END, lambda: gather_sums(OWN, 1, part, INNER, OWN_X, OWN_Y))
        within(MID, lambda: gather_sums(OWN, 1, part, OUTER, OWN_X, OWN_Y, OWN_INNER))
    gu_grad(2)
    gather_sums(ACROSS, 0, 1, TO_X)
    gather_sums(ALONG, 0, 0, TO_Y)
    gather_sums(ACROSS, 0, 0, TO_X, ACROSS_Y)
    gather_sums(ALONG, 0, 1, TO_Y, ALONG_X)
    gu_grad(3)

    def finish_sums(*boxes):
        gate_sums = []
        for part in range(2):
            value = part_ref[mine, core, piece(part)].astype(jnp.float32)
            for box in boxes:
                value = value + incoming(OWN, 0, part, box)
            tokens_out[piece(part), :] = value[:, :features].astype(jnp.bfloat16)
            gate_sums.append(value[:, features:])
        sums = jnp.concatenate(gate_sums, axis=0).T
        picked = jnp.zeros(routing.shape, jnp.float32)
        for index in range(experts):
            picked = jnp.where(routing == index, sums[index : index + 1], picked)
        gates_out[...] = jnp.where(usable, picked, 0.0)

    within(END, lambda: finish_sums(OWN_X, OWN_Y, OWN_INNER))
    within(MID, lambda: finish_sums(OWN_X, OWN_Y, OWN_INNER, OWN_OUTER))

    def settle(role):
        for make, args in unsent[role]:
            make(*args).wait_send()

    settle(ALL)
    within(END, lambda: settle(END))
    within(MID, lambda: settle(MID))


def finish_kernel(*refs):
    count = (len(refs) - 1) // 2
    copies = [
        pltpu.make_async_copy(refs[index], refs[count + index], refs[-1].at[index])
        for index in range(count)
    ]
    for copy in copies:
        copy.start()
    for copy in copies:
        copy.wait()


def fused_layer(tokens, grad_out, routing, replica, gates, host_expert, w_gate_up, w_down):
    count, features = tokens.shape
    owned, quarter = w_down.shape[:2]
    size = lax.axis_size("expert")
    experts = owned * size
    depth = size // 2
    chips = 4 * depth
    lanes = (experts + 127) // 128 * 128
    kind = jnp.bfloat16
    width, sums = 2 * features + lanes, features + lanes
    outside = pl.BlockSpec(memory_space=pltpu.HBM)
    inside = pl.BlockSpec(memory_space=pltpu.VMEM)
    boxes = 8 * depth * 2
    turned = (routing.shape[1], count)
    results = (
        ((count, features), kind),
        (turned, jnp.float32),
        (w_gate_up.shape, kind),
        (w_down.shape, kind),
    )
    held = pl.pallas_call(
        functools.partial(fused_kernel, experts),
        out_shape=tuple(pltpu.VMEM(*result) for result in results),
        in_specs=[outside] * 8,
        out_specs=(inside,) * 4,
        scratch_shapes=[
            pltpu.VMEM((chips, 2, count, width), kind),
            pltpu.VMEM(w_gate_up.shape, kind),
            pltpu.VMEM(w_down.shape, kind),
            pltpu.VMEM((2 * owned, chips, 2 * count, quarter), kind),
            pltpu.VMEM((owned, chips, 2 * count, quarter), kind),
            pltpu.VMEM((chips, 2, count, sums), kind),
            pltpu.VMEM((chips, count, sums), kind),
            pltpu.VMEM((boxes, count // 2, sums), kind),
            pltpu.VMEM(turned, jnp.int32),
            pltpu.VMEM(turned, jnp.int32),
            pltpu.VMEM(turned, kind),
            pltpu.SMEM(host_expert.shape, jnp.int32),
            pltpu.SemaphoreType.DMA((8,)),
            pltpu.SemaphoreType.DMA((chips, 10)),
            pltpu.SemaphoreType.DMA((chips, 2, 2)),
            pltpu.SemaphoreType.DMA((chips,)),
            pltpu.SemaphoreType.DMA((chips,)),
            pltpu.SemaphoreType.DMA((boxes,)),
            pltpu.SemaphoreType.DMA((boxes,)),
        ],
        compiler_params=pltpu.CompilerParams(
            collective_id=0, has_side_effects=True, vmem_limit_bytes=44 << 20
        ),
    )(
        *(
            pltpu.with_memory_space_constraint(value, pltpu.HBM)
            for value in (
                tokens, grad_out, routing.T, replica.T, gates.T, host_expert, w_gate_up, w_down
            )
        )
    )
    return pl.pallas_call(
        finish_kernel,
        out_shape=tuple(jax.ShapeDtypeStruct(*result) for result in results),
        in_specs=[inside] * 4,
        out_specs=(outside,) * 4,
        scratch_shapes=[pltpu.SemaphoreType.DMA((4,))],
        compiler_params=pltpu.CompilerParams(vmem_limit_bytes=1 << 20),
    )(*held)


def gathered_shards(
    tokens, grad_out, routing, replica, gates, host_expert, w_gate_up, w_down
):
    grad_tokens, grad_gates, grad_gu, grad_down = fused_layer(
        tokens, grad_out, routing, replica, gates, host_expert, w_gate_up, w_down
    )
    return (grad_tokens, grad_gates.T, grad_gu, grad_down)


def serve(tokens, grad_out, routing, replica, gates, host_expert, w_gate_up, w_down):
    grid = lax.axis_size("dp") == 4 and lax.axis_size("expert") == 8
    visits_all = routing.shape[1] >= lax.axis_size("expert")
    body = gathered_shards if grid and visits_all else shards
    return body(tokens, grad_out, routing, replica, gates, host_expert, w_gate_up, w_down)


def solution(mesh):
    in_specs = (
        P(("dp", "expert"), None),
        P(("dp", "expert"), None),
        P(("dp", "expert"), None),
        P(("dp", "expert"), None),
        P(("dp", "expert"), None),
        P(),
        P("expert", None, "dp", None),
        P("expert", "dp", None),
    )
    out_specs = (
        P(("dp", "expert"), None),
        P(("dp", "expert"), None),
        P("expert", None, "dp", None),
        P("expert", "dp", None),
    )
    return jax.shard_map(serve, mesh=mesh, in_specs=in_specs, out_specs=out_specs, check_vma=False)
```

```python
import functools

import jax
import jax.numpy as jnp
from jax import lax
from jax.experimental import pallas as pl
from jax.experimental.pallas import tpu as pltpu
from jax.sharding import PartitionSpec as P

MESH = pl.DeviceIdType.MESH


def lookup(values_table, indices):
    matches = indices[..., None] == lax.broadcasted_iota(
        jnp.int32, indices.shape + values_table.shape, indices.ndim
    )
    return jnp.sum(jnp.where(matches, values_table, 0), axis=-1)


def placement(host_expert, owned_experts, devices):
    experts = owned_experts * devices
    matches = host_expert[None, :] == lax.broadcasted_iota(jnp.int32, (experts, devices), 0)
    helper_ids = lax.broadcasted_iota(jnp.int32, (experts, devices), 1)
    helper_of = jnp.sum(jnp.where(matches, helper_ids, 0), axis=1)
    listed = jnp.sum(matches.astype(jnp.int32), axis=1)
    return (helper_of, listed)


def targets(routing, replica, host_expert, owned_experts, devices, slot_rows, groups):
    helper_of, listed = placement(host_expert, owned_experts, devices)
    choices = routing.shape[0] // groups * routing.shape[1]
    usable = (replica == 0) | (lookup(listed, routing) > 0)
    device_to = jnp.where(replica == 0, routing // owned_experts, lookup(helper_of, routing))
    block_to = jnp.where(replica == 0, routing % owned_experts, owned_experts)
    labels = (routing * 2 + replica).reshape(groups, choices)
    earlier = lax.broadcasted_iota(jnp.int32, (choices, choices), 1) < lax.broadcasted_iota(
        jnp.int32, (choices, choices), 0
    )
    matching = (labels[:, :, None] == labels[:, None, :]) & earlier[None]
    ranking = jnp.sum(matching.astype(jnp.int32), axis=2).reshape(routing.shape)
    group_ids = lax.broadcasted_iota(jnp.int32, (groups, choices), 0).reshape(routing.shape)
    position = ((block_to * groups + group_ids) * devices + device_to) * slot_rows + ranking
    return jnp.where(usable, position, -1)


def selector(position, total_slots):
    matches = position[None, :, :] == lax.broadcasted_iota(
        jnp.int32, (total_slots,) + position.shape, 0
    )
    picker = jnp.sum(matches.astype(jnp.float32), axis=2).astype(jnp.bfloat16)
    return (matches, picker)


def fill_rows(matches, picker, tokens, grad_out, gates):
    row_x = jnp.dot(picker, tokens, preferred_element_type=jnp.float32).astype(jnp.bfloat16)
    row_dy = jnp.dot(picker, grad_out, preferred_element_type=jnp.float32).astype(jnp.bfloat16)
    row_gate = jnp.sum(
        jnp.where(matches, gates[None].astype(jnp.float32), 0.0), axis=(1, 2)
    ).astype(jnp.bfloat16)
    return (row_x, row_dy, row_gate)


def expert_block(inputs, upstream, weight, gate_up, down_matrix):
    mixed = jnp.einsum("rd,jfd->jrf", inputs, gate_up, preferred_element_type=jnp.float32)
    gate_pre = mixed[0]
    up_part = mixed[1]
    sigmoid_gate = jax.nn.sigmoid(gate_pre)
    active = gate_pre * sigmoid_gate
    hidden = (active * up_part).astype(jnp.bfloat16)
    output_part = jnp.einsum("rf,fd->rd", hidden, down_matrix, preferred_element_type=jnp.float32)
    gate_part = jnp.sum(output_part * upstream.astype(jnp.float32), axis=1)
    scaled = (weight.astype(jnp.float32)[:, None] * upstream.astype(jnp.float32)).astype(
        jnp.bfloat16
    )
    grad_hidden = jnp.einsum("rd,fd->rf", scaled, down_matrix, preferred_element_type=jnp.float32)
    grad_gate = grad_hidden * up_part * sigmoid_gate * (1.0 + gate_pre * (1.0 - sigmoid_gate))
    grad_mixed = jnp.stack([grad_gate, grad_hidden * active], axis=0).astype(jnp.bfloat16)
    input_part = jnp.einsum("jrf,jfd->rd", grad_mixed, gate_up, preferred_element_type=jnp.float32)
    weight_gu = jnp.einsum("jrf,rd->jfd", grad_mixed, inputs, preferred_element_type=jnp.float32)
    weight_down = jnp.einsum("rf,rd->fd", hidden, scaled, preferred_element_type=jnp.float32)
    return (input_part, gate_part, weight_gu, weight_down)


def shards(tokens, grad_out, routing, replica, gates, host_expert, w_gate_up, w_down):
    devices = lax.axis_size("expert")
    device_id = lax.axis_index("expert")
    token_rows, features = tokens.shape
    owned_experts = w_gate_up.shape[0]
    quarter = w_down.shape[1]
    topk_width = routing.shape[1]
    slot_rows = token_rows * topk_width // (owned_experts * devices)
    blocks = owned_experts + 1
    lane_rows = devices * slot_rows
    piece_rows = quarter // devices
    home_slots = targets(routing, replica, host_expert, owned_experts, devices, slot_rows, 1)
    home_matches, home_picker = selector(home_slots, blocks * lane_rows)
    row_x, row_dy, row_gate = fill_rows(home_matches, home_picker, tokens, grad_out, gates)
    sent_x, sent_dy, sent_gate = (
        lax.all_to_all(
            row_x.reshape(blocks, lane_rows, features),
            "expert",
            split_axis=1,
            concat_axis=1,
            tiled=True,
        ),
        lax.all_to_all(
            row_dy.reshape(blocks, lane_rows, features),
            "expert",
            split_axis=1,
            concat_axis=1,
            tiled=True,
        ),
        lax.all_to_all(
            row_gate.reshape(blocks, lane_rows), "expert", split_axis=1, concat_axis=1, tiled=True
        ),
    )
    block_x, block_dy, block_gate = (
        lax.all_gather(sent_x, "dp", axis=1, tiled=True),
        lax.all_gather(sent_dy, "dp", axis=1, tiled=True),
        lax.all_gather(sent_gate, "dp", axis=1, tiled=True),
    )
    owner_of_helper = host_expert // owned_experts
    owns_copy = owner_of_helper == device_id
    copied_local = jnp.sum(jnp.where(owns_copy, host_expert % owned_experts, 0))
    helper_ids = lax.broadcasted_iota(jnp.int32, (devices, devices), 1)
    owner_ids = lax.broadcasted_iota(jnp.int32, (devices, devices), 0)
    helper_of_owner = jnp.sum(
        jnp.where(owner_of_helper[None, :] == owner_ids, helper_ids, 0), axis=1
    )
    source_gu = lax.dynamic_index_in_dim(w_gate_up, copied_local, 0, keepdims=False)
    source_down = lax.dynamic_index_in_dim(w_down, copied_local, 0, keepdims=False)
    spread_gu, spread_down = (
        lax.all_to_all(
            source_gu.reshape(2, devices, piece_rows, features),
            "expert",
            split_axis=1,
            concat_axis=1,
            tiled=True,
        ),
        lax.all_to_all(
            source_down.reshape(1, devices, piece_rows, features),
            "expert",
            split_axis=1,
            concat_axis=1,
            tiled=True,
        ),
    )
    spread_gu = jnp.take(spread_gu, owner_of_helper, axis=1)
    spread_down = jnp.take(spread_down, owner_of_helper, axis=1)
    hosted_gu, hosted_down = (
        lax.all_to_all(spread_gu, "expert", split_axis=1, concat_axis=1, tiled=True),
        lax.all_to_all(spread_down, "expert", split_axis=1, concat_axis=1, tiled=True),
    )
    hosted_gu = hosted_gu.reshape(2, quarter, features)
    hosted_down = hosted_down.reshape(quarter, features)
    input_parts = []
    gate_parts = []
    owner_gu = []
    owner_down = []
    for block in range(blocks):
        if block < owned_experts:
            gate_up = w_gate_up[block]
            down_matrix = w_down[block]
        else:
            gate_up = hosted_gu
            down_matrix = hosted_down
        input_part, gate_part, weight_gu, weight_down = expert_block(
            block_x[block], block_dy[block], block_gate[block], gate_up, down_matrix
        )
        input_parts.append(input_part.astype(jnp.bfloat16))
        gate_parts.append(gate_part.astype(jnp.bfloat16))
        owner_gu.append(weight_gu)
        owner_down.append(weight_down)
    helper_gu = owner_gu[owned_experts].astype(jnp.bfloat16)
    helper_down = owner_down[owned_experts].astype(jnp.bfloat16)
    back_gu, back_down = (
        lax.all_to_all(
            helper_gu.reshape(2, devices, piece_rows, features),
            "expert",
            split_axis=1,
            concat_axis=1,
            tiled=True,
        ),
        lax.all_to_all(
            helper_down.reshape(1, devices, piece_rows, features),
            "expert",
            split_axis=1,
            concat_axis=1,
            tiled=True,
        ),
    )
    back_gu = jnp.take(back_gu, helper_of_owner, axis=1)
    back_down = jnp.take(back_down, helper_of_owner, axis=1)
    extra_gu, extra_down = (
        lax.all_to_all(back_gu, "expert", split_axis=1, concat_axis=1, tiled=True),
        lax.all_to_all(back_down, "expert", split_axis=1, concat_axis=1, tiled=True),
    )
    extra_gu = extra_gu.reshape(2, quarter, features).astype(jnp.float32)
    extra_down = extra_down.reshape(quarter, features).astype(jnp.float32)
    stacked_dx = jnp.stack(input_parts, axis=0)
    stacked_dg = jnp.stack(gate_parts, axis=0)
    summed_dx, summed_dg = (
        lax.psum_scatter(stacked_dx, "dp", scatter_dimension=1, tiled=True).astype(jnp.float32),
        lax.psum_scatter(stacked_dg, "dp", scatter_dimension=1, tiled=True).astype(jnp.float32),
    )
    row_dx = summed_dx.astype(jnp.bfloat16)
    row_dg = summed_dg.astype(jnp.bfloat16)
    home_dx, home_dg = (
        lax.all_to_all(row_dx, "expert", split_axis=1, concat_axis=1, tiled=True),
        lax.all_to_all(row_dg, "expert", split_axis=1, concat_axis=1, tiled=True),
    )
    home_dx = home_dx.reshape(blocks * lane_rows, features)
    home_dg = home_dg.reshape(blocks * lane_rows).astype(jnp.float32)
    grad_tokens = jnp.einsum(
        "st,sd->td", home_picker, home_dx, preferred_element_type=jnp.float32
    ).astype(jnp.bfloat16)
    grad_gates = jnp.sum(jnp.where(home_matches, home_dg[:, None, None], 0.0), axis=0)
    grad_gu = []
    grad_down = []
    for block in range(owned_experts):
        present = (copied_local == block).astype(jnp.float32)
        grad_gu.append((owner_gu[block] + present * extra_gu).astype(jnp.bfloat16))
        grad_down.append((owner_down[block] + present * extra_down).astype(jnp.bfloat16))
    return (grad_tokens, grad_gates, jnp.stack(grad_gu, axis=0), jnp.stack(grad_down, axis=0))


OWN, ACROSS, ALONG, DIAGONAL = range(4)
PARTNER, TO_X, TO_Y, INNER, OUTER, FAR_MID, FAR_END = range(7)
OWN_X, OWN_Y, OWN_INNER, OWN_OUTER, OWN_FAR_MID, OWN_FAR_END = range(6)
ACROSS_Y, ALONG_X, DIAGONAL_INNER, DIAGONAL_OUTER = range(6, 10)
BOXES = 10
END, MID = range(2)

GROUPS = (
    ((OWN, 0), (OWN, 1), (ACROSS, 0), (ALONG, 0),),
    ((DIAGONAL, 0), (OWN, 2), (ACROSS, 1), (ALONG, 1),),
    ((OWN, 3), (ACROSS, 2), (ALONG, 2), (DIAGONAL, 2),),
    ((DIAGONAL, 3), (DIAGONAL, 1),),
    ((ACROSS, 3), (ALONG, 3),),
)
ARRIVE, SEND, COMBINE, SUM = range(1, 5)
WHOLE = 2

SCHEDULE = (
    (
        (
            20001, 20012, 20003, 20002, 20013, 20011, 12010, 11000, 22011, 21002,
            10110, 20112, 20020, 10100, 20111, 13000, 12000, 20101, 10210, 13010,
            23003, 20102, 11010, 10200, 20202, 22020, 11110, 20120, 23013, 12110,
            21020, 20211, 20220, 20201, 20212,
        ),
        (
            10300, 11100, 23020, 12100, 22120, 12200, 21102, 21120, 10310, 22111,
        ),
        (
            20302,
        ),
        (
            20320, 20301, 20312, 11200, 13200, 20311, 32000, 30100, 12210, 30000,
            31000, 41010, 22220, 11210, 21220, 13210, 23220,
        ),
        (),
        (),
        (
            13110, 31100, 12300, 13300, 32100, 13100, 30200, 42100, 23120, 41110,
            13310, 23320, 31200, 11310, 41200, 33200, 12310, 43200, 11300, 22320,
            32200, 42200, 41210, 42210, 21320,
        ),
        (),
        (
            43210, 33300, 43310, 43300,
        ),
        (
            33100, 43100, 43110,
        ),
        (
            40200, 33000, 40210, 31300, 32300, 42300, 41300, 42310, 43000, 41310,
            41100, 43010, 30300,
        ),
        (
            40300, 42110,
        ),
        (
            40310, 42000, 41000, 40100,
        ),
        (
            42010, 40110,
        ),
        (),
        (
            40000, 40010,
        ),
    ),
    (
        (
            20004, 20013, 20001, 20011, 20014, 20003, 20012, 20002, 10100, 10210,
            11000, 12010, 21002, 22011, 20103, 20214, 10110, 11010, 20101, 10200,
            20111, 20113, 20102, 20112, 20202, 20204, 13000, 20212, 20211, 12000,
            10300, 20201, 20304, 23003, 20120, 21020, 20220, 22020, 12100, 10310,
            20020, 13010, 20314, 23013, 11100, 13100, 13200, 23020, 20320, 20301,
            12110, 11110, 23204, 20311, 20302, 23103,
        ),
        (
            22120, 20312, 13110, 21120, 23113, 23120, 13210, 23214,
        ),
        (),
        (
            12200, 11210, 12210, 32000, 11200, 13300, 21220, 22220, 23304, 23220,
            30000, 42000,
        ),
        (
            31000, 13310, 23314,
        ),
        (
            23320, 11300,
        ),
        (
            12300, 32100, 11310, 21320, 42100, 12310, 31100, 42110, 22320,
        ),
        (),
        (
            41110, 33200, 33300, 43300, 43310, 41100,
        ),
        (),
        (
            30100, 43200, 33100, 31200, 43100, 31300, 32300, 42300, 41300, 43110,
            42310, 41310,
        ),
        (
            41200, 43210, 33000, 32200, 42200, 40110, 30200, 42210, 30300, 43000,
            40300, 40100, 41210, 40310,
        ),
        (
            40200, 43010, 41000,
        ),
        (
            40210, 42010, 41010,
        ),
        (
            40000,
        ),
        (
            40010,
        ),
    ),
)


PLACES = sum(GROUPS, ())
SWAPPED = (1, 0, 2, 3)
CROSSED = (2, 3, 0, 1)


def place(role, near):
    return PLACES.index((role, near))


def seen_from(kind, way, role, near):
    if way == TO_X:
        return role ^ 1, near
    if way == TO_Y:
        return role ^ 2, near
    if way == PARTNER:
        return role, near
    if way == FAR_MID or way == FAR_END:
        return role, 3 - near
    return role, (CROSSED if kind == MID and way == INNER else SWAPPED)[near]


def within_plane(kind, near):
    return near == 0 or near == 3 or (near == 1 and kind == END)


def parent(kind, role, near, part):
    if role == ACROSS:
        return TO_X
    if role == ALONG:
        return TO_Y
    if role == DIAGONAL and within_plane(kind, near):
        return (TO_Y, TO_X)[part]
    if role == OWN and near == 0:
        return None
    if near == 3:
        return FAR_END
    return OUTER if kind == MID and near == 1 else INNER


def children(kind, role, near, part):
    if role == ACROSS:
        return (ACROSS_Y,) if part == 0 and within_plane(kind, near) else ()
    if role == ALONG:
        return (ALONG_X,) if part == 1 and within_plane(kind, near) else ()
    if role == DIAGONAL:
        if near == 0:
            return (DIAGONAL_INNER,)
        return (DIAGONAL_OUTER,) if kind == MID and near == 2 else ()
    boxes = (OWN_X, OWN_Y)
    if near == 0:
        boxes += (OWN_INNER,)
        boxes += (OWN_FAR_MID, OWN_FAR_END) if kind == END else (OWN_OUTER,)
    if near == 2 and kind == MID:
        boxes += (OWN_OUTER,)
    return boxes


def usable_choices(routing, replica, host_ref):
    usable = replica == 0
    for index in range(host_ref.shape[0]):
        usable = usable | (routing == host_ref[index])
    return usable


def fused_kernel(
    experts,
    tokens_hbm,
    grad_out_hbm,
    routing_hbm,
    replica_hbm,
    gates_hbm,
    host_hbm,
    gu_hbm,
    down_hbm,
    tokens_out,
    gates_out,
    grad_gu_ref,
    grad_down_ref,
    rows_ref,
    gu_ref,
    down_ref,
    mixed_ref,
    hidden_ref,
    part_ref,
    paired_ref,
    inbox_ref,
    gate_sums_ref,
    routing_ref,
    replica_ref,
    gates_ref,
    host_ref,
    local,
    sent,
    landed,
    pair_sent,
    pair_landed,
    sums_sent,
    sums_landed,
):
    dp = lax.axis_index("dp")
    expert = lax.axis_index("expert")
    height, core = expert // 2, expert % 2
    row, column = dp // 2, dp % 2
    depth = rows_ref.shape[0] // 4
    count = rows_ref.shape[2]
    half = count // 2
    features = tokens_hbm.shape[1]
    lanes = rows_ref.shape[3] - 2 * features
    owned, quarter = down_hbm.shape[:2]
    hidden_units = owned * quarter
    across = row * 2 + 1 - column
    along = (1 - row) * 2 + column
    upper = height // (depth // 2)
    outer_level = height + 1 - 2 * (height % 2)
    is_mid = (height + upper) % 2 == 1
    is_end = (height + upper) % 2 == 0
    inner_level = height + 1 - 2 * upper
    targets_of = (
        (dp, height * 2 + 1 - core),
        (across, expert),
        (along, expert),
        (dp, inner_level * 2 + core),
        (dp, outer_level * 2 + core),
        (dp, (depth // 2 - upper) * 2 + core),
        (dp, (depth - 1) * (1 - upper) * 2 + core),
    )
    kinds = [None]
    unsent = ([], [])
    shared = []

    def within(kind, body):
        kinds[0] = kind

        @pl.when(is_end if kind == END else is_mid)
        def _():
            body()

        kinds[0] = None

    def begin(make, *args):
        make(*args).start()
        (shared if kinds[0] is None else unsent[kinds[0]]).append((make, args))

    mine = place(OWN, 0)
    loads = [
        pltpu.make_async_copy(routing_hbm, routing_ref, local.at[0]),
        pltpu.make_async_copy(replica_hbm, replica_ref, local.at[1]),
        pltpu.make_async_copy(gates_hbm, gates_ref, local.at[2]),
        pltpu.make_async_copy(host_hbm, host_ref, local.at[3]),
        pltpu.make_async_copy(tokens_hbm, rows_ref.at[mine, core, :, pl.ds(0, features)], local.at[4]),
        pltpu.make_async_copy(
            grad_out_hbm, rows_ref.at[mine, core, :, pl.ds(features, features)], local.at[5]
        ),
    ]
    for index in range(2 * owned):
        loads.append(
            pltpu.make_async_copy(
                gu_hbm.at[index % owned, index // owned],
                gu_ref.at[pl.ds(index * quarter, quarter)],
                local.at[6 + index],
            )
        )
    for index in range(owned):
        loads.append(
            pltpu.make_async_copy(
                down_hbm.at[index],
                down_ref.at[pl.ds(index * quarter, quarter)],
                local.at[6 + 2 * owned + index],
            )
        )
    for load in loads:
        load.start()
    barrier = pltpu.get_barrier_semaphore()
    for kind, ways in ((END, (FAR_MID,)), (MID, (OUTER,))):

        @pl.when(is_end if kind == END else is_mid)
        def _():
            for way in (PARTNER, TO_X, TO_Y, INNER, FAR_END) + ways:
                pl.semaphore_signal(
                    barrier, inc=1, device_id=targets_of[way], device_id_type=MESH
                )

    for load in loads[:4]:
        load.wait()
    routing = routing_ref[...]
    usable = usable_choices(routing, replica_ref[...], host_ref)
    gates = jnp.where(usable, gates_ref[...].astype(jnp.float32), 0.0)
    weights = jnp.concatenate(
        [
            jnp.sum(jnp.where(routing == index, gates, 0.0), axis=0, keepdims=True)
            for index in range(experts)
        ]
        + [jnp.zeros((lanes - experts, count), jnp.float32)],
        axis=0,
    )
    rows_ref[mine, core, :, 2 * features :] = weights.T.astype(jnp.bfloat16)
    for load in loads[4:6]:
        load.wait()
    pl.semaphore_wait(barrier, 6)

    def piece(part):
        return pl.ds(part * half, half)

    def row_copy(role, near, part, way):
        at, to = place(role, near), place(*seen_from(kinds[0], way, role, near))
        span = slice(None) if part is None else piece(part)
        index = 0 if part is None else part
        return pltpu.make_async_remote_copy(
            src_ref=rows_ref.at[at, core, span],
            dst_ref=rows_ref.at[to, core, span],
            send_sem=sent.at[at, way * 2 + index],
            recv_sem=landed.at[to, core, index],
            device_id=targets_of[way],
            device_id_type=MESH,
        )

    def partner_rows(role, near):
        at = place(role, near)
        block = rows_ref.at[at, 1 - core]
        pltpu.make_async_remote_copy(
            src_ref=block,
            dst_ref=block,
            send_sem=sent.at[at, 0],
            recv_sem=landed.at[at, 1 - core, 0],
            device_id=targets_of[PARTNER],
            device_id_type=MESH,
        ).wait_recv()

    def rows_by_columns(a, b):
        return lax.dot_general(
            a, b, (((1,), (1,)), ((), ())), preferred_element_type=jnp.float32
        )

    def columns_by_columns(a, b):
        return lax.dot_general(
            a, b, (((0,), (0,)), ((), ())), preferred_element_type=jnp.float32
        ).astype(jnp.bfloat16)

    chip_rows = 2 * count

    def pair_copy(at):
        return pltpu.make_async_remote_copy(
            src_ref=part_ref.at[at, 1 - core],
            dst_ref=paired_ref.at[at],
            send_sem=pair_sent.at[at],
            recv_sem=pair_landed.at[at],
            device_id=targets_of[PARTNER],
            device_id_type=MESH,
        )

    def stacked(ref, index, first, size):
        group = GROUPS[index]
        start = place(*group[0])
        rows = ref[start : start + len(group), ..., first : first + size]
        return rows.reshape(len(group) * chip_rows, size)

    def keep(ref, index, first, values):
        start, stop = place(*GROUPS[index][0]), place(*GROUPS[index][-1]) + 1
        size = values.shape[1]
        shape = (stop - start,) + ref.shape[1:-1] + (size,)
        ref[start:stop, ..., first : first + size] = values.reshape(shape)

    def ahead(group):
        for role, near in GROUPS[group]:
            partner_rows(role, near)
        side = stacked(rows_ref, group, 2 * features, lanes).astype(jnp.float32)
        slots = lax.broadcasted_iota(jnp.int32, side.shape, 1)
        shape = (side.shape[0], hidden_units)
        units = lax.broadcasted_iota(jnp.int32, shape, 1)
        at_expert = [slots == expert * owned + index for index in range(owned)]
        of_expert = [
            (units >= index * quarter) & (units < (index + 1) * quarter) for index in range(owned)
        ]
        weight = jnp.zeros(shape, jnp.float32)
        for index in range(owned):
            scale = jnp.sum(jnp.where(at_expert[index], side, 0.0), axis=1, keepdims=True)
            weight = jnp.where(of_expert[index], scale, weight)
        mixed = rows_by_columns(stacked(rows_ref, group, 0, features), gu_ref[...])
        raw_hidden = rows_by_columns(stacked(rows_ref, group, features, features), down_ref[...])
        gate_pre = mixed[:, :hidden_units]
        up_part = mixed[:, hidden_units:]
        sigmoid_gate = jax.nn.sigmoid(gate_pre)
        active = gate_pre * sigmoid_gate
        hidden = (active * up_part).astype(jnp.bfloat16).astype(jnp.float32)
        gate_parts = hidden * raw_hidden
        gate_side = jnp.zeros(side.shape, jnp.float32)
        for index in range(owned):
            total = jnp.sum(
                jnp.where(of_expert[index], gate_parts, 0.0), axis=1, keepdims=True
            )
            gate_side = jnp.where(at_expert[index], total, gate_side)
        grad_hidden = raw_hidden * weight
        grad_gate = (
            grad_hidden * up_part * sigmoid_gate * (1.0 + gate_pre * (1.0 - sigmoid_gate))
        ).astype(jnp.bfloat16)
        grad_up = (grad_hidden * active).astype(jnp.bfloat16)
        weighted = (hidden * weight).astype(jnp.bfloat16)
        gate_side = gate_side.astype(jnp.bfloat16)
        keep(hidden_ref, group, 0, weighted)
        keep(mixed_ref, group, 0, grad_gate)
        keep(mixed_ref, group, hidden_units, grad_up)
        keep(part_ref, group, features, gate_side)

    def back(group):
        dx = jnp.dot(
            stacked(mixed_ref, group, 0, 2 * hidden_units),
            gu_ref[...],
            preferred_element_type=jnp.float32,
        )
        keep(part_ref, group, 0, dx.astype(jnp.bfloat16))
        for role, near in GROUPS[group]:
            begin(pair_copy, place(role, near))

    def combine(role, near):
        at = place(role, near)
        pair_copy(at).wait_recv()
        part_ref[at, core] = (
            part_ref[at, core].astype(jnp.float32) + paired_ref[at].astype(jnp.float32)
        ).astype(jnp.bfloat16)

    def box_index(box, near, part):
        return (box * depth + near) * 2 + part

    def sum_copy(role, near, part, way, box):
        index = box_index(box, seen_from(kinds[0], way, role, near)[1], part)
        return pltpu.make_async_remote_copy(
            src_ref=part_ref.at[place(role, near), core, piece(part)],
            dst_ref=inbox_ref.at[index],
            send_sem=sums_sent.at[box_index(box, near, part)],
            recv_sem=sums_landed.at[index],
            device_id=targets_of[way],
            device_id_type=MESH,
        )

    def incoming(role, near, part, box):
        index = box_index(box, near, part)
        pltpu.make_async_remote_copy(
            src_ref=inbox_ref.at[index],
            dst_ref=inbox_ref.at[index],
            send_sem=sums_sent.at[index],
            recv_sem=sums_landed.at[index],
            device_id=targets_of[PARTNER],
            device_id_type=MESH,
        ).wait_recv()
        return inbox_ref[index].astype(jnp.float32)

    def home_box(role, way):
        if way == TO_X:
            return ALONG_X if role == DIAGONAL else OWN_X
        if way == TO_Y:
            return ACROSS_Y if role == DIAGONAL else OWN_Y
        if way == FAR_END:
            return OWN_FAR_END if kinds[0] == END else OWN_FAR_MID
        if kinds[0] == END:
            return OWN_OUTER if role == OWN else DIAGONAL_OUTER
        return OWN_INNER if role == OWN else DIAGONAL_INNER

    def gather_sums(role, near, part):
        kind = kinds[0]
        at = place(role, near)
        boxes, way = children(kind, role, near, part), parent(kind, role, near, part)
        if boxes:
            value = part_ref[at, core, piece(part)].astype(jnp.float32)
            for box in boxes:
                value = value + incoming(role, near, part, box)
            if way is None:
                tokens_out[piece(part), :] = value[:, :features].astype(jnp.bfloat16)
                gate_sums_ref[piece(part), :] = value[:, features:]
            else:
                part_ref[at, core, piece(part)] = value.astype(jnp.bfloat16)
        if way is not None:
            begin(sum_copy, role, near, part, way, home_box(role, way))

    total_rows = 4 * depth * chip_rows

    def weight_grad(ref, out_ref, source, first, size):
        sources = rows_ref[:, :, :, source * features : (source + 1) * features]
        grads = columns_by_columns(
            ref[:, :, first : first + size].reshape(total_rows, size),
            sources.reshape(total_rows, features),
        )
        start = first
        while start < first + size:
            index, offset = start // quarter, start % quarter
            taken = min(quarter - offset, first + size - start)
            where = (index % owned, index // owned) if source == 0 else (index,)
            out_ref[where + (pl.ds(offset, taken),)] = grads[start - first : start - first + taken]
            start += taken

    jobs = []
    for first in range(0, 2 * hidden_units, 256):
        size = min(256, 2 * hidden_units - first)
        jobs.append((mixed_ref, grad_gu_ref, 0, first, size))
    for first in range(0, hidden_units, 256):
        size = min(256, hidden_units - first)
        jobs.append((hidden_ref, grad_down_ref, 1, first, size))

    def play(codes):
        for code in codes:
            action, role, near, part, way = (code // 10**place_of % 10 for place_of in range(4, -1, -1))
            part = None if part == WHOLE else part
            if action == ARRIVE:
                row_copy(role, near, part, PARTNER).wait_recv()
            elif action == SEND:
                begin(row_copy, role, near, part, way)
            elif action == COMBINE:
                combine(role, near)
            else:
                gather_sums(role, near, part)

    stages = []
    for group in range(len(GROUPS)):
        stages.append((ahead, (group,)))
        stages.append((back, (group,)))
    stages += [(weight_grad, job) for job in jobs]
    for index, codes in enumerate(zip(*SCHEDULE, strict=True)):
        for kind in (END, MID):
            if codes[kind]:
                within(kind, functools.partial(play, codes[kind]))
        if index == 0:
            for load in loads[6:]:
                load.wait()
        if index < len(stages):
            stages[index][0](*stages[index][1])
    sums = gate_sums_ref[...].T
    picked = jnp.zeros(routing.shape, jnp.float32)
    for index in range(experts):
        picked = jnp.where(routing == index, sums[index : index + 1], picked)
    gates_out[...] = jnp.where(usable, picked, 0.0)

    def settle(sends):
        for make, args in sends:
            make(*args).wait_send()

    settle(shared)
    within(END, lambda: settle(unsent[END]))
    within(MID, lambda: settle(unsent[MID]))


def finish_kernel(*refs):
    count = (len(refs) - 1) // 2
    copies = [
        pltpu.make_async_copy(refs[index], refs[count + index], refs[-1].at[index])
        for index in range(count)
    ]
    for copy in copies:
        copy.start()
    for copy in copies:
        copy.wait()


def fused_layer(tokens, grad_out, routing, replica, gates, host_expert, w_gate_up, w_down):
    count, features = tokens.shape
    owned, quarter = w_down.shape[:2]
    size = lax.axis_size("expert")
    experts = owned * size
    depth = size // 2
    chips = 4 * depth
    lanes = (experts + 127) // 128 * 128
    kind = jnp.bfloat16
    width, sums = 2 * features + lanes, features + lanes
    outside = pl.BlockSpec(memory_space=pltpu.HBM)
    inside = pl.BlockSpec(memory_space=pltpu.VMEM)
    boxes = BOXES * depth * 2
    units = owned * quarter
    turned = (routing.shape[1], count)
    results = (
        ((count, features), kind),
        (turned, jnp.float32),
        (w_gate_up.shape, kind),
        (w_down.shape, kind),
    )
    held = pl.pallas_call(
        functools.partial(fused_kernel, experts),
        out_shape=tuple(pltpu.VMEM(*result) for result in results),
        in_specs=[outside] * 8,
        out_specs=(inside,) * 4,
        scratch_shapes=[
            pltpu.VMEM((chips, 2, count, width), kind),
            pltpu.VMEM((2 * units, features), kind),
            pltpu.VMEM((units, features), kind),
            pltpu.VMEM((chips, 2 * count, 2 * units), kind),
            pltpu.VMEM((chips, 2 * count, units), kind),
            pltpu.VMEM((chips, 2, count, sums), kind),
            pltpu.VMEM((chips, count, sums), kind),
            pltpu.VMEM((boxes, count // 2, sums), kind),
            pltpu.VMEM((count, lanes), jnp.float32),
            pltpu.VMEM(turned, jnp.int32),
            pltpu.VMEM(turned, jnp.int32),
            pltpu.VMEM(turned, kind),
            pltpu.SMEM(host_expert.shape, jnp.int32),
            pltpu.SemaphoreType.DMA((6 + 3 * owned,)),
            pltpu.SemaphoreType.DMA((chips, 14)),
            pltpu.SemaphoreType.DMA((chips, 2, 2)),
            pltpu.SemaphoreType.DMA((chips,)),
            pltpu.SemaphoreType.DMA((chips,)),
            pltpu.SemaphoreType.DMA((boxes,)),
            pltpu.SemaphoreType.DMA((boxes,)),
        ],
        compiler_params=pltpu.CompilerParams(
            collective_id=0, has_side_effects=True, vmem_limit_bytes=44 << 20
        ),
    )(
        *(
            pltpu.with_memory_space_constraint(value, pltpu.HBM)
            for value in (
                tokens, grad_out, routing.T, replica.T, gates.T, host_expert, w_gate_up, w_down
            )
        )
    )
    return pl.pallas_call(
        finish_kernel,
        out_shape=tuple(jax.ShapeDtypeStruct(*result) for result in results),
        in_specs=[inside] * 4,
        out_specs=(outside,) * 4,
        scratch_shapes=[pltpu.SemaphoreType.DMA((4,))],
        compiler_params=pltpu.CompilerParams(vmem_limit_bytes=1 << 20),
    )(*held)


def gathered_shards(
    tokens, grad_out, routing, replica, gates, host_expert, w_gate_up, w_down
):
    grad_tokens, grad_gates, grad_gu, grad_down = fused_layer(
        tokens, grad_out, routing, replica, gates, host_expert, w_gate_up, w_down
    )
    return (grad_tokens, grad_gates.T, grad_gu, grad_down)


def serve(tokens, grad_out, routing, replica, gates, host_expert, w_gate_up, w_down):
    grid = lax.axis_size("dp") == 4 and lax.axis_size("expert") == 8
    visits_all = routing.shape[1] >= lax.axis_size("expert")
    body = gathered_shards if grid and visits_all else shards
    return body(tokens, grad_out, routing, replica, gates, host_expert, w_gate_up, w_down)


def solution(mesh):
    in_specs = (
        P(("dp", "expert"), None),
        P(("dp", "expert"), None),
        P(("dp", "expert"), None),
        P(("dp", "expert"), None),
        P(("dp", "expert"), None),
        P(),
        P("expert", None, "dp", None),
        P("expert", "dp", None),
    )
    out_specs = (
        P(("dp", "expert"), None),
        P(("dp", "expert"), None),
        P("expert", None, "dp", None),
        P("expert", "dp", None),
    )
    return jax.shard_map(serve, mesh=mesh, in_specs=in_specs, out_specs=out_specs, check_vma=False)
```

```python
import functools

import jax
import jax.numpy as jnp
from jax import lax
from jax.experimental import pallas as pl
from jax.experimental.pallas import tpu as pltpu
from jax.sharding import PartitionSpec as P

MESH = pl.DeviceIdType.MESH


def lookup(values_table, indices):
    matches = indices[..., None] == lax.broadcasted_iota(
        jnp.int32, indices.shape + values_table.shape, indices.ndim
    )
    return jnp.sum(jnp.where(matches, values_table, 0), axis=-1)


def placement(host_expert, owned_experts, devices):
    experts = owned_experts * devices
    matches = host_expert[None, :] == lax.broadcasted_iota(jnp.int32, (experts, devices), 0)
    helper_ids = lax.broadcasted_iota(jnp.int32, (experts, devices), 1)
    helper_of = jnp.sum(jnp.where(matches, helper_ids, 0), axis=1)
    listed = jnp.sum(matches.astype(jnp.int32), axis=1)
    return (helper_of, listed)


def targets(routing, replica, host_expert, owned_experts, devices, slot_rows, groups):
    helper_of, listed = placement(host_expert, owned_experts, devices)
    choices = routing.shape[0] // groups * routing.shape[1]
    usable = (replica == 0) | (lookup(listed, routing) > 0)
    device_to = jnp.where(replica == 0, routing // owned_experts, lookup(helper_of, routing))
    block_to = jnp.where(replica == 0, routing % owned_experts, owned_experts)
    labels = (routing * 2 + replica).reshape(groups, choices)
    earlier = lax.broadcasted_iota(jnp.int32, (choices, choices), 1) < lax.broadcasted_iota(
        jnp.int32, (choices, choices), 0
    )
    matching = (labels[:, :, None] == labels[:, None, :]) & earlier[None]
    ranking = jnp.sum(matching.astype(jnp.int32), axis=2).reshape(routing.shape)
    group_ids = lax.broadcasted_iota(jnp.int32, (groups, choices), 0).reshape(routing.shape)
    position = ((block_to * groups + group_ids) * devices + device_to) * slot_rows + ranking
    return jnp.where(usable, position, -1)


def selector(position, total_slots):
    matches = position[None, :, :] == lax.broadcasted_iota(
        jnp.int32, (total_slots,) + position.shape, 0
    )
    picker = jnp.sum(matches.astype(jnp.float32), axis=2).astype(jnp.bfloat16)
    return (matches, picker)


def fill_rows(matches, picker, tokens, grad_out, gates):
    row_x = jnp.dot(picker, tokens, preferred_element_type=jnp.float32).astype(jnp.bfloat16)
    row_dy = jnp.dot(picker, grad_out, preferred_element_type=jnp.float32).astype(jnp.bfloat16)
    row_gate = jnp.sum(
        jnp.where(matches, gates[None].astype(jnp.float32), 0.0), axis=(1, 2)
    ).astype(jnp.bfloat16)
    return (row_x, row_dy, row_gate)


def expert_block(inputs, upstream, weight, gate_up, down_matrix):
    mixed = jnp.einsum("rd,jfd->jrf", inputs, gate_up, preferred_element_type=jnp.float32)
    gate_pre = mixed[0]
    up_part = mixed[1]
    sigmoid_gate = jax.nn.sigmoid(gate_pre)
    active = gate_pre * sigmoid_gate
    hidden = (active * up_part).astype(jnp.bfloat16)
    output_part = jnp.einsum("rf,fd->rd", hidden, down_matrix, preferred_element_type=jnp.float32)
    gate_part = jnp.sum(output_part * upstream.astype(jnp.float32), axis=1)
    scaled = (weight.astype(jnp.float32)[:, None] * upstream.astype(jnp.float32)).astype(
        jnp.bfloat16
    )
    grad_hidden = jnp.einsum("rd,fd->rf", scaled, down_matrix, preferred_element_type=jnp.float32)
    grad_gate = grad_hidden * up_part * sigmoid_gate * (1.0 + gate_pre * (1.0 - sigmoid_gate))
    grad_mixed = jnp.stack([grad_gate, grad_hidden * active], axis=0).astype(jnp.bfloat16)
    input_part = jnp.einsum("jrf,jfd->rd", grad_mixed, gate_up, preferred_element_type=jnp.float32)
    weight_gu = jnp.einsum("jrf,rd->jfd", grad_mixed, inputs, preferred_element_type=jnp.float32)
    weight_down = jnp.einsum("rf,rd->fd", hidden, scaled, preferred_element_type=jnp.float32)
    return (input_part, gate_part, weight_gu, weight_down)


def shards(tokens, grad_out, routing, replica, gates, host_expert, w_gate_up, w_down):
    devices = lax.axis_size("expert")
    device_id = lax.axis_index("expert")
    token_rows, features = tokens.shape
    owned_experts = w_gate_up.shape[0]
    quarter = w_down.shape[1]
    topk_width = routing.shape[1]
    slot_rows = token_rows * topk_width // (owned_experts * devices)
    blocks = owned_experts + 1
    lane_rows = devices * slot_rows
    piece_rows = quarter // devices
    home_slots = targets(routing, replica, host_expert, owned_experts, devices, slot_rows, 1)
    home_matches, home_picker = selector(home_slots, blocks * lane_rows)
    row_x, row_dy, row_gate = fill_rows(home_matches, home_picker, tokens, grad_out, gates)
    sent_x, sent_dy, sent_gate = (
        lax.all_to_all(
            row_x.reshape(blocks, lane_rows, features),
            "expert",
            split_axis=1,
            concat_axis=1,
            tiled=True,
        ),
        lax.all_to_all(
            row_dy.reshape(blocks, lane_rows, features),
            "expert",
            split_axis=1,
            concat_axis=1,
            tiled=True,
        ),
        lax.all_to_all(
            row_gate.reshape(blocks, lane_rows), "expert", split_axis=1, concat_axis=1, tiled=True
        ),
    )
    block_x, block_dy, block_gate = (
        lax.all_gather(sent_x, "dp", axis=1, tiled=True),
        lax.all_gather(sent_dy, "dp", axis=1, tiled=True),
        lax.all_gather(sent_gate, "dp", axis=1, tiled=True),
    )
    owner_of_helper = host_expert // owned_experts
    owns_copy = owner_of_helper == device_id
    copied_local = jnp.sum(jnp.where(owns_copy, host_expert % owned_experts, 0))
    helper_ids = lax.broadcasted_iota(jnp.int32, (devices, devices), 1)
    owner_ids = lax.broadcasted_iota(jnp.int32, (devices, devices), 0)
    helper_of_owner = jnp.sum(
        jnp.where(owner_of_helper[None, :] == owner_ids, helper_ids, 0), axis=1
    )
    source_gu = lax.dynamic_index_in_dim(w_gate_up, copied_local, 0, keepdims=False)
    source_down = lax.dynamic_index_in_dim(w_down, copied_local, 0, keepdims=False)
    spread_gu, spread_down = (
        lax.all_to_all(
            source_gu.reshape(2, devices, piece_rows, features),
            "expert",
            split_axis=1,
            concat_axis=1,
            tiled=True,
        ),
        lax.all_to_all(
            source_down.reshape(1, devices, piece_rows, features),
            "expert",
            split_axis=1,
            concat_axis=1,
            tiled=True,
        ),
    )
    spread_gu = jnp.take(spread_gu, owner_of_helper, axis=1)
    spread_down = jnp.take(spread_down, owner_of_helper, axis=1)
    hosted_gu, hosted_down = (
        lax.all_to_all(spread_gu, "expert", split_axis=1, concat_axis=1, tiled=True),
        lax.all_to_all(spread_down, "expert", split_axis=1, concat_axis=1, tiled=True),
    )
    hosted_gu = hosted_gu.reshape(2, quarter, features)
    hosted_down = hosted_down.reshape(quarter, features)
    input_parts = []
    gate_parts = []
    owner_gu = []
    owner_down = []
    for block in range(blocks):
        if block < owned_experts:
            gate_up = w_gate_up[block]
            down_matrix = w_down[block]
        else:
            gate_up = hosted_gu
            down_matrix = hosted_down
        input_part, gate_part, weight_gu, weight_down = expert_block(
            block_x[block], block_dy[block], block_gate[block], gate_up, down_matrix
        )
        input_parts.append(input_part.astype(jnp.bfloat16))
        gate_parts.append(gate_part.astype(jnp.bfloat16))
        owner_gu.append(weight_gu)
        owner_down.append(weight_down)
    helper_gu = owner_gu[owned_experts].astype(jnp.bfloat16)
    helper_down = owner_down[owned_experts].astype(jnp.bfloat16)
    back_gu, back_down = (
        lax.all_to_all(
            helper_gu.reshape(2, devices, piece_rows, features),
            "expert",
            split_axis=1,
            concat_axis=1,
            tiled=True,
        ),
        lax.all_to_all(
            helper_down.reshape(1, devices, piece_rows, features),
            "expert",
            split_axis=1,
            concat_axis=1,
            tiled=True,
        ),
    )
    back_gu = jnp.take(back_gu, helper_of_owner, axis=1)
    back_down = jnp.take(back_down, helper_of_owner, axis=1)
    extra_gu, extra_down = (
        lax.all_to_all(back_gu, "expert", split_axis=1, concat_axis=1, tiled=True),
        lax.all_to_all(back_down, "expert", split_axis=1, concat_axis=1, tiled=True),
    )
    extra_gu = extra_gu.reshape(2, quarter, features).astype(jnp.float32)
    extra_down = extra_down.reshape(quarter, features).astype(jnp.float32)
    stacked_dx = jnp.stack(input_parts, axis=0)
    stacked_dg = jnp.stack(gate_parts, axis=0)
    summed_dx, summed_dg = (
        lax.psum_scatter(stacked_dx, "dp", scatter_dimension=1, tiled=True).astype(jnp.float32),
        lax.psum_scatter(stacked_dg, "dp", scatter_dimension=1, tiled=True).astype(jnp.float32),
    )
    row_dx = summed_dx.astype(jnp.bfloat16)
    row_dg = summed_dg.astype(jnp.bfloat16)
    home_dx, home_dg = (
        lax.all_to_all(row_dx, "expert", split_axis=1, concat_axis=1, tiled=True),
        lax.all_to_all(row_dg, "expert", split_axis=1, concat_axis=1, tiled=True),
    )
    home_dx = home_dx.reshape(blocks * lane_rows, features)
    home_dg = home_dg.reshape(blocks * lane_rows).astype(jnp.float32)
    grad_tokens = jnp.einsum(
        "st,sd->td", home_picker, home_dx, preferred_element_type=jnp.float32
    ).astype(jnp.bfloat16)
    grad_gates = jnp.sum(jnp.where(home_matches, home_dg[:, None, None], 0.0), axis=0)
    grad_gu = []
    grad_down = []
    for block in range(owned_experts):
        present = (copied_local == block).astype(jnp.float32)
        grad_gu.append((owner_gu[block] + present * extra_gu).astype(jnp.bfloat16))
        grad_down.append((owner_down[block] + present * extra_down).astype(jnp.bfloat16))
    return (grad_tokens, grad_gates, jnp.stack(grad_gu, axis=0), jnp.stack(grad_down, axis=0))


OWN, ACROSS, ALONG, DIAGONAL = range(4)
PARTNER, TO_X, TO_Y, INNER, OUTER, FAR_MID, FAR_END = range(7)
OWN_X, OWN_Y, OWN_INNER, OWN_OUTER, OWN_FAR_MID, OWN_FAR_END = range(6)
ACROSS_Y, ALONG_X, ACROSS_OUTER, ALONG_OUTER, DIAGONAL_INNER, DIAGONAL_OUTER = range(6, 12)
BOXES = 12
OUTER_BOXES = (OWN_OUTER, ACROSS_OUTER, ALONG_OUTER, DIAGONAL_OUTER)
END, MID = range(2)

GROUPS = (
    ((OWN, 0), (OWN, 1), (ACROSS, 0), (ALONG, 0),),
    ((DIAGONAL, 0), (OWN, 2), (ACROSS, 1), (ALONG, 1),),
    ((OWN, 3), (ACROSS, 2), (ALONG, 2), (DIAGONAL, 2),),
    ((DIAGONAL, 3), (DIAGONAL, 1),),
    ((ACROSS, 3), (ALONG, 3),),
)
ARRIVE, SEND, COMBINE, SUM = range(1, 5)
WHOLE = 2

SCHEDULE = (
    (
        (
            20001, 20020, 20003, 20012, 20013, 20011, 20002, 12010, 11000, 22011,
            21002, 10100, 11010, 20101, 20102, 13000, 10110, 12000, 21020, 20112,
            13010, 10210, 20120, 20111, 23013, 20212, 20211, 22020, 23020, 23003,
            10200, 12100, 20220, 20201,
        ),
        (
            12110, 22120, 20202, 11100, 11110, 21120,
        ),
        (
            22111,
        ),
        (
            10310, 20311, 12210, 21102, 10300, 20302, 30100, 32000, 20312,
        ),
        (
            20301, 20320, 11200, 40110, 31100, 42000, 11210, 12200, 22220, 31000,
            21220, 32100, 13200, 42100, 13210, 23220, 13110, 13100, 41110, 41100,
        ),
        (),
        (
            33000, 23120, 30000, 30300, 11310, 42110, 31200, 13310, 41200, 32200,
            13300, 23320, 42200, 11300, 41010, 21320, 42210, 12300, 30200, 12310,
            33200, 22320, 41210, 43210, 43200,
        ),
        (),
        (
            40200, 33300, 43300, 43310, 33100, 43110,
        ),
        (),
        (
            43100, 40210, 31300, 41300, 32300, 42300, 42310, 41310,
        ),
        (
            43010, 43000, 40300,
        ),
        (
            40310,
        ),
        (
            40100, 42010, 41000,
        ),
        (),
        (
            40000, 40010,
        ),
    ),
    (
        (
            20014, 20001, 20013, 20012, 20020, 20003, 20002, 20004, 20011, 11000,
            10210, 12010, 10100, 22011, 20103, 21002, 20214, 10200, 10110, 12000,
            20112, 20101, 20204, 11010, 20111, 21020, 20113, 20102, 20202, 20201,
            22020, 10300, 20304, 20120, 13000, 13010, 23003,
        ),
        (
            23013, 20220, 20212, 20302, 23020, 10310, 20314, 11100,
        ),
        (
            20211, 11110, 21120, 12100, 12110, 20301, 13110, 13200, 22120, 31000,
            30000, 23113, 20320, 23204,
        ),
        (
            13210, 13100, 23220, 12200, 23103, 23214, 20311,
        ),
        (
            20312, 11210, 11200, 21220, 12210, 30100, 13310, 22220, 31100, 23314,
            32100, 23120, 41110,
        ),
        (
            11300, 13300, 23304, 42110, 41100, 23320,
        ),
        (),
        (
            12310, 12300,
        ),
        (
            31200, 11310, 21320, 32000, 41200, 42100, 30200, 22320, 33300, 43310,
            32200, 33100, 41010, 30300, 43300, 43100,
        ),
        (
            42200,
        ),
        (
            32300, 43110, 42300, 33200, 31300, 43210, 42310, 41300, 40100, 40110,
            43200, 42210, 41310, 40200, 33000, 40300, 43010,
        ),
        (
            41210, 40310, 43000, 42010,
        ),
        (
            42000, 41000, 40210,
        ),
        (),
        (),
        (
            40000, 40010,
        ),
    ),
)


PLACES = sum(GROUPS, ())
SWAPPED = (1, 0, 2, 3)
CROSSED = (2, 3, 0, 1)


def place(role, near):
    return PLACES.index((role, near))


def seen_from(kind, way, role, near):
    if way == TO_X:
        return role ^ 1, near
    if way == TO_Y:
        return role ^ 2, near
    if way == PARTNER:
        return role, near
    if way == FAR_MID or way == FAR_END:
        return role, 3 - near
    return role, (CROSSED if kind == MID and way == INNER else SWAPPED)[near]


def parent(kind, role, near, part):
    if kind == END and near == 1:
        return INNER
    if role == ACROSS:
        return TO_X
    if role == ALONG:
        return TO_Y
    if role == DIAGONAL and (near == 0 or near == 3):
        return (TO_Y, TO_X)[part]
    if near == 0:
        return None
    if near == 3:
        return FAR_END
    return OUTER if near == 1 else INNER


def children(kind, role, near, part):
    if kind == END and near == 1:
        return ()
    fed = kind == MID and (near == 0 or (near == 2 and role in (OWN, DIAGONAL)))
    boxes = (OUTER_BOXES[role],) if fed else ()
    if role == ACROSS or role == ALONG:
        sided = (near == 0 or near == 3) and part == (0 if role == ACROSS else 1)
        return boxes + ((ACROSS_Y if role == ACROSS else ALONG_X,) if sided else ())
    if role == DIAGONAL:
        return boxes + ((DIAGONAL_INNER,) if near == 0 else ())
    boxes += (OWN_X, OWN_Y)
    if near == 0:
        boxes += (OWN_INNER,)
        if kind == END:
            boxes += (OWN_FAR_MID, OWN_FAR_END)
    return boxes


def usable_choices(routing, replica, host_ref):
    usable = replica == 0
    for index in range(host_ref.shape[0]):
        usable = usable | (routing == host_ref[index])
    return usable


def fused_kernel(
    experts,
    tokens_hbm,
    grad_out_hbm,
    routing_hbm,
    replica_hbm,
    gates_hbm,
    host_hbm,
    gu_hbm,
    down_hbm,
    tokens_out,
    gates_out,
    grad_gu_ref,
    grad_down_ref,
    rows_ref,
    gu_ref,
    down_ref,
    gu_turned_ref,
    down_turned_ref,
    mixed_ref,
    hidden_ref,
    part_ref,
    paired_ref,
    inbox_ref,
    gate_sums_ref,
    routing_ref,
    replica_ref,
    gates_ref,
    host_ref,
    local,
    sent,
    landed,
    pair_sent,
    pair_landed,
    sums_sent,
    sums_landed,
):
    dp = lax.axis_index("dp")
    expert = lax.axis_index("expert")
    height, core = expert // 2, expert % 2
    row, column = dp // 2, dp % 2
    depth = rows_ref.shape[0] // 4
    count = rows_ref.shape[2]
    half = count // 2
    features = tokens_hbm.shape[1]
    lanes = rows_ref.shape[3] - 2 * features
    owned, quarter = down_hbm.shape[:2]
    hidden_units = owned * quarter
    across = row * 2 + 1 - column
    along = (1 - row) * 2 + column
    upper = height // (depth // 2)
    outer_level = height + 1 - 2 * (height % 2)
    is_mid = (height + upper) % 2 == 1
    is_end = (height + upper) % 2 == 0
    inner_level = height + 1 - 2 * upper
    targets_of = (
        (dp, height * 2 + 1 - core),
        (across, expert),
        (along, expert),
        (dp, inner_level * 2 + core),
        (dp, outer_level * 2 + core),
        (dp, (depth // 2 - upper) * 2 + core),
        (dp, (depth - 1) * (1 - upper) * 2 + core),
    )
    kinds = [None]
    unsent = ([], [])
    shared = []

    def within(kind, body):
        kinds[0] = kind

        @pl.when(is_end if kind == END else is_mid)
        def _():
            body()

        kinds[0] = None

    def begin(make, *args):
        make(*args).start()
        (shared if kinds[0] is None else unsent[kinds[0]]).append((make, args))

    mine = place(OWN, 0)
    loads = [
        pltpu.make_async_copy(routing_hbm, routing_ref, local.at[0]),
        pltpu.make_async_copy(replica_hbm, replica_ref, local.at[1]),
        pltpu.make_async_copy(gates_hbm, gates_ref, local.at[2]),
        pltpu.make_async_copy(host_hbm, host_ref, local.at[3]),
        pltpu.make_async_copy(tokens_hbm, rows_ref.at[mine, core, :, pl.ds(0, features)], local.at[4]),
        pltpu.make_async_copy(
            grad_out_hbm, rows_ref.at[mine, core, :, pl.ds(features, features)], local.at[5]
        ),
    ]
    for index in range(2 * owned):
        loads.append(
            pltpu.make_async_copy(
                gu_hbm.at[index % owned, index // owned],
                gu_ref.at[pl.ds(index * quarter, quarter)],
                local.at[6 + index],
            )
        )
    for index in range(owned):
        loads.append(
            pltpu.make_async_copy(
                down_hbm.at[index],
                down_ref.at[pl.ds(index * quarter, quarter)],
                local.at[6 + 2 * owned + index],
            )
        )
    for load in loads[:6]:
        load.start()
    barrier = pltpu.get_barrier_semaphore()
    for kind, ways in ((END, (FAR_MID,)), (MID, (OUTER,))):

        @pl.when(is_end if kind == END else is_mid)
        def _():
            for way in (PARTNER, TO_X, TO_Y, INNER, FAR_END) + ways:
                pl.semaphore_signal(
                    barrier, inc=1, device_id=targets_of[way], device_id_type=MESH
                )

    for load in loads[:4]:
        load.wait()
    routing = routing_ref[...]
    usable = usable_choices(routing, replica_ref[...], host_ref)
    gates = jnp.where(usable, gates_ref[...].astype(jnp.float32), 0.0)
    weights = jnp.concatenate(
        [
            jnp.sum(jnp.where(routing == index, gates, 0.0), axis=0, keepdims=True)
            for index in range(experts)
        ]
        + [jnp.zeros((lanes - experts, count), jnp.float32)],
        axis=0,
    )
    weights = weights.T
    side = weights[:half] + pltpu.roll(weights[half:], lanes // 2, 1)
    rows_ref[mine, core, :half, 2 * features :] = side.astype(jnp.bfloat16)
    for load in loads[4:6]:
        load.wait()
    pl.semaphore_wait(barrier, 6)
    for load in loads[6:]:
        load.start()

    def piece(part):
        return pl.ds(part * half, half)

    def span_of(part, width):
        return pl.ds(0, width + lanes if part == 0 else width)

    def row_copy(role, near, part, way):
        at, to = place(role, near), place(*seen_from(kinds[0], way, role, near))
        if part is None:
            span = (slice(None), slice(None))
        else:
            span = (piece(part), span_of(part, 2 * features))
        index = 0 if part is None else part
        return pltpu.make_async_remote_copy(
            src_ref=rows_ref.at[(at, core) + span],
            dst_ref=rows_ref.at[(to, core) + span],
            send_sem=sent.at[at, way * 2 + index],
            recv_sem=landed.at[to, core, index],
            device_id=targets_of[way],
            device_id_type=MESH,
        )

    def partner_rows(role, near):
        at = place(role, near)
        block = rows_ref.at[at, 1 - core]
        pltpu.make_async_remote_copy(
            src_ref=block,
            dst_ref=block,
            send_sem=sent.at[at, 0],
            recv_sem=landed.at[at, 1 - core, 0],
            device_id=targets_of[PARTNER],
            device_id_type=MESH,
        ).wait_recv()

    def rows_by_rows(a, b):
        return jnp.dot(a, b, preferred_element_type=jnp.float32)

    def columns_by_columns(a, b):
        return lax.dot_general(
            a, b, (((0,), (0,)), ((), ())), preferred_element_type=jnp.float32
        ).astype(jnp.bfloat16)

    chip_rows = 2 * count

    def pair_copy(at):
        return pltpu.make_async_remote_copy(
            src_ref=part_ref.at[at, 1 - core],
            dst_ref=paired_ref.at[at],
            send_sem=pair_sent.at[at],
            recv_sem=pair_landed.at[at],
            device_id=targets_of[PARTNER],
            device_id_type=MESH,
        )

    def stacked(ref, index, first, size):
        group = GROUPS[index]
        start = place(*group[0])
        rows = ref[start : start + len(group), ..., first : first + size]
        return rows.reshape(len(group) * chip_rows, size)

    def keep(ref, index, first, values):
        start, stop = place(*GROUPS[index][0]), place(*GROUPS[index][-1]) + 1
        size = values.shape[1]
        shape = (stop - start,) + ref.shape[1:-1] + (size,)
        ref[start:stop, ..., first : first + size] = values.reshape(shape)

    def ahead(group):
        for role, near in GROUPS[group]:
            partner_rows(role, near)
        start, size = place(*GROUPS[group][0]), len(GROUPS[group])
        packed = rows_ref[start : start + size, :, :half, 2 * features :].astype(jnp.float32)
        packed = packed.reshape(2 * size * half, lanes)
        turned = pltpu.roll(packed, lanes // 2, 1)
        side = jnp.concatenate(
            [packed.reshape(2 * size, half, lanes), turned.reshape(2 * size, half, lanes)], axis=1
        ).reshape(2 * size * count, lanes)
        slots = lax.broadcasted_iota(jnp.int32, side.shape, 1)
        shape = (side.shape[0], hidden_units)
        units = lax.broadcasted_iota(jnp.int32, shape, 1)
        at_expert = [slots == expert * owned + index for index in range(owned)]
        of_expert = [
            (units >= index * quarter) & (units < (index + 1) * quarter) for index in range(owned)
        ]
        weight = jnp.zeros(shape, jnp.float32)
        for index in range(owned):
            scale = jnp.sum(jnp.where(at_expert[index], side, 0.0), axis=1, keepdims=True)
            weight = jnp.where(of_expert[index], scale, weight)
        mixed = rows_by_rows(stacked(rows_ref, group, 0, features), gu_turned_ref[...])
        raw_hidden = rows_by_rows(stacked(rows_ref, group, features, features), down_turned_ref[...])
        gate_pre = mixed[:, :hidden_units]
        up_part = mixed[:, hidden_units:]
        sigmoid_gate = jax.nn.sigmoid(gate_pre)
        active = gate_pre * sigmoid_gate
        hidden = (active * up_part).astype(jnp.bfloat16).astype(jnp.float32)
        gate_parts = hidden * raw_hidden
        gate_side = jnp.zeros(side.shape, jnp.float32)
        for index in range(owned):
            total = jnp.sum(
                jnp.where(of_expert[index], gate_parts, 0.0), axis=1, keepdims=True
            )
            gate_side = jnp.where(at_expert[index], total, gate_side)
        grad_hidden = raw_hidden * weight
        grad_gate = (
            grad_hidden * up_part * sigmoid_gate * (1.0 + gate_pre * (1.0 - sigmoid_gate))
        ).astype(jnp.bfloat16)
        grad_up = (grad_hidden * active).astype(jnp.bfloat16)
        weighted = (hidden * weight).astype(jnp.bfloat16)
        gate_side = gate_side.reshape(2 * size, count, lanes)
        low = gate_side[:, :half].reshape(2 * size * half, lanes)
        high = gate_side[:, half:].reshape(2 * size * half, lanes)
        packed = (low + pltpu.roll(high, lanes // 2, 1)).astype(jnp.bfloat16)
        part_ref[start : start + size, :, :half, features:] = packed.reshape(
            size, 2, half, lanes
        )
        keep(hidden_ref, group, 0, weighted)
        keep(mixed_ref, group, 0, grad_gate)
        keep(mixed_ref, group, hidden_units, grad_up)

    def back(group):
        dx = jnp.dot(
            stacked(mixed_ref, group, 0, 2 * hidden_units),
            gu_ref[...],
            preferred_element_type=jnp.float32,
        )
        keep(part_ref, group, 0, dx.astype(jnp.bfloat16))
        for role, near in GROUPS[group]:
            begin(pair_copy, place(role, near))

    def combine(role, near):
        at = place(role, near)
        pair_copy(at).wait_recv()
        for part in range(2):
            span = (piece(part), span_of(part, features))
            part_ref[(at, core) + span] = (
                part_ref[(at, core) + span].astype(jnp.float32)
                + paired_ref[(at,) + span].astype(jnp.float32)
            ).astype(jnp.bfloat16)

    def box_index(box, near, part):
        return (box * depth + near) * 2 + part

    def sum_copy(role, near, part, way, box):
        index = box_index(box, seen_from(kinds[0], way, role, near)[1], part)
        width = span_of(part, features)
        return pltpu.make_async_remote_copy(
            src_ref=part_ref.at[place(role, near), core, piece(part), width],
            dst_ref=inbox_ref.at[index, :, width],
            send_sem=sums_sent.at[box_index(box, near, part)],
            recv_sem=sums_landed.at[index],
            device_id=targets_of[way],
            device_id_type=MESH,
        )

    def incoming(role, near, part, box):
        index = box_index(box, near, part)
        width = span_of(part, features)
        pltpu.make_async_remote_copy(
            src_ref=inbox_ref.at[index, :, width],
            dst_ref=inbox_ref.at[index, :, width],
            send_sem=sums_sent.at[index],
            recv_sem=sums_landed.at[index],
            device_id=targets_of[PARTNER],
            device_id_type=MESH,
        ).wait_recv()
        return inbox_ref[index, :, width].astype(jnp.float32)

    def home_box(role, way):
        if way == TO_X:
            return ALONG_X if role == DIAGONAL else OWN_X
        if way == TO_Y:
            return ACROSS_Y if role == DIAGONAL else OWN_Y
        if way == FAR_END:
            return OWN_FAR_END if kinds[0] == END else OWN_FAR_MID
        if kinds[0] == END:
            return OUTER_BOXES[role]
        return OWN_INNER if role == OWN else DIAGONAL_INNER

    def gather_sums(role, near, part):
        kind = kinds[0]
        at = place(role, near)
        boxes, way = children(kind, role, near, part), parent(kind, role, near, part)
        if boxes:
            span = (piece(part), span_of(part, features))
            value = part_ref[(at, core) + span].astype(jnp.float32)
            for box in boxes:
                value = value + incoming(role, near, part, box)
            if way is None:
                tokens_out[piece(part), :] = value[:, :features].astype(jnp.bfloat16)
                if part == 0:
                    gate_sums_ref[...] = value[:, features:]
            else:
                part_ref[(at, core) + span] = value.astype(jnp.bfloat16)
        if way is not None:
            begin(sum_copy, role, near, part, way, home_box(role, way))

    total_rows = 4 * depth * chip_rows

    def weight_grad(ref, out_ref, source, first, size):
        sources = rows_ref[:, :, :, source * features : (source + 1) * features]
        grads = columns_by_columns(
            ref[:, :, first : first + size].reshape(total_rows, size),
            sources.reshape(total_rows, features),
        )
        start = first
        while start < first + size:
            index, offset = start // quarter, start % quarter
            taken = min(quarter - offset, first + size - start)
            where = (index % owned, index // owned) if source == 0 else (index,)
            out_ref[where + (pl.ds(offset, taken),)] = grads[start - first : start - first + taken]
            start += taken

    jobs = []
    for first in range(0, 2 * hidden_units, 256):
        size = min(256, 2 * hidden_units - first)
        jobs.append((mixed_ref, grad_gu_ref, 0, first, size))
    for first in range(0, hidden_units, 256):
        size = min(256, hidden_units - first)
        jobs.append((hidden_ref, grad_down_ref, 1, first, size))

    def play(codes):
        for code in codes:
            action, role, near, part, way = (code // 10**place_of % 10 for place_of in range(4, -1, -1))
            part = None if part == WHOLE else part
            if action == ARRIVE:
                row_copy(role, near, part, PARTNER).wait_recv()
            elif action == SEND:
                begin(row_copy, role, near, part, way)
            elif action == COMBINE:
                combine(role, near)
            else:
                gather_sums(role, near, part)

    stages = []
    for group in range(len(GROUPS)):
        stages.append((ahead, (group,)))
        stages.append((back, (group,)))
    stages += [(weight_grad, job) for job in jobs]
    def opening(codes):
        return next(index for index, code in enumerate(codes) if code // 10000 == ARRIVE)

    for kind in (END, MID):
        codes = SCHEDULE[kind][0]
        within(kind, functools.partial(play, codes[: opening(codes)]))
    for load in loads[6:]:
        load.wait()
    for ref, turned_ref in ((gu_ref, gu_turned_ref), (down_ref, down_turned_ref)):
        for first in range(0, features, 512):
            turned_ref[first : first + 512, :] = ref[:, first : first + 512].T
    for index, codes in enumerate(zip(*SCHEDULE, strict=True)):
        for kind in (END, MID):
            steps = codes[kind][opening(codes[kind]) :] if index == 0 else codes[kind]
            if steps:
                within(kind, functools.partial(play, steps))
        if index < len(stages):
            stages[index][0](*stages[index][1])
    packed = gate_sums_ref[...]
    sums = jnp.concatenate([packed, pltpu.roll(packed, lanes // 2, 1)], axis=0).T
    picked = jnp.zeros(routing.shape, jnp.float32)
    for index in range(experts):
        picked = jnp.where(routing == index, sums[index : index + 1], picked)
    gates_out[...] = jnp.where(usable, picked, 0.0)

    def settle(sends):
        for make, args in sends:
            make(*args).wait_send()

    settle(shared)
    within(END, lambda: settle(unsent[END]))
    within(MID, lambda: settle(unsent[MID]))


def finish_kernel(*refs):
    count = (len(refs) - 1) // 2
    copies = [
        pltpu.make_async_copy(refs[index], refs[count + index], refs[-1].at[index])
        for index in range(count)
    ]
    for copy in copies:
        copy.start()
    for copy in copies:
        copy.wait()


def fused_layer(tokens, grad_out, routing, replica, gates, host_expert, w_gate_up, w_down):
    count, features = tokens.shape
    owned, quarter = w_down.shape[:2]
    size = lax.axis_size("expert")
    experts = owned * size
    depth = size // 2
    chips = 4 * depth
    lanes = (2 * experts + 127) // 128 * 128
    kind = jnp.bfloat16
    width, sums = 2 * features + lanes, features + lanes
    outside = pl.BlockSpec(memory_space=pltpu.HBM)
    inside = pl.BlockSpec(memory_space=pltpu.VMEM)
    boxes = BOXES * depth * 2
    units = owned * quarter
    turned = (routing.shape[1], count)
    results = (
        ((count, features), kind),
        (turned, jnp.float32),
        (w_gate_up.shape, kind),
        (w_down.shape, kind),
    )
    held = pl.pallas_call(
        functools.partial(fused_kernel, experts),
        out_shape=tuple(pltpu.VMEM(*result) for result in results),
        in_specs=[outside] * 8,
        out_specs=(inside,) * 4,
        scratch_shapes=[
            pltpu.VMEM((chips, 2, count, width), kind),
            pltpu.VMEM((2 * units, features), kind),
            pltpu.VMEM((units, features), kind),
            pltpu.VMEM((features, 2 * units), kind),
            pltpu.VMEM((features, units), kind),
            pltpu.VMEM((chips, 2 * count, 2 * units), kind),
            pltpu.VMEM((chips, 2 * count, units), kind),
            pltpu.VMEM((chips, 2, count, sums), kind),
            pltpu.VMEM((chips, count, sums), kind),
            pltpu.VMEM((boxes, count // 2, sums), kind),
            pltpu.VMEM((count // 2, lanes), jnp.float32),
            pltpu.VMEM(turned, jnp.int32),
            pltpu.VMEM(turned, jnp.int32),
            pltpu.VMEM(turned, kind),
            pltpu.SMEM(host_expert.shape, jnp.int32),
            pltpu.SemaphoreType.DMA((6 + 3 * owned,)),
            pltpu.SemaphoreType.DMA((chips, 14)),
            pltpu.SemaphoreType.DMA((chips, 2, 2)),
            pltpu.SemaphoreType.DMA((chips,)),
            pltpu.SemaphoreType.DMA((chips,)),
            pltpu.SemaphoreType.DMA((boxes,)),
            pltpu.SemaphoreType.DMA((boxes,)),
        ],
        compiler_params=pltpu.CompilerParams(
            collective_id=0, has_side_effects=True, vmem_limit_bytes=44 << 20
        ),
    )(
        *(
            pltpu.with_memory_space_constraint(value, pltpu.HBM)
            for value in (
                tokens, grad_out, routing.T, replica.T, gates.T, host_expert, w_gate_up, w_down
            )
        )
    )
    return pl.pallas_call(
        finish_kernel,
        out_shape=tuple(jax.ShapeDtypeStruct(*result) for result in results),
        in_specs=[inside] * 4,
        out_specs=(outside,) * 4,
        scratch_shapes=[pltpu.SemaphoreType.DMA((4,))],
        compiler_params=pltpu.CompilerParams(vmem_limit_bytes=1 << 20),
    )(*held)


def gathered_shards(
    tokens, grad_out, routing, replica, gates, host_expert, w_gate_up, w_down
):
    grad_tokens, grad_gates, grad_gu, grad_down = fused_layer(
        tokens, grad_out, routing, replica, gates, host_expert, w_gate_up, w_down
    )
    return (grad_tokens, grad_gates.T, grad_gu, grad_down)


def serve(tokens, grad_out, routing, replica, gates, host_expert, w_gate_up, w_down):
    grid = lax.axis_size("dp") == 4 and lax.axis_size("expert") == 8
    visits_all = routing.shape[1] >= lax.axis_size("expert")
    body = gathered_shards if grid and visits_all else shards
    return body(tokens, grad_out, routing, replica, gates, host_expert, w_gate_up, w_down)


def solution(mesh):
    in_specs = (
        P(("dp", "expert"), None),
        P(("dp", "expert"), None),
        P(("dp", "expert"), None),
        P(("dp", "expert"), None),
        P(("dp", "expert"), None),
        P(),
        P("expert", None, "dp", None),
        P("expert", "dp", None),
    )
    out_specs = (
        P(("dp", "expert"), None),
        P(("dp", "expert"), None),
        P("expert", None, "dp", None),
        P("expert", "dp", None),
    )
    return jax.shard_map(serve, mesh=mesh, in_specs=in_specs, out_specs=out_specs, check_vma=False)
```

```python
import functools

import jax
import jax.numpy as jnp
from jax import lax
from jax.experimental import pallas as pl
from jax.experimental.pallas import tpu as pltpu
from jax.sharding import PartitionSpec as P

MESH = pl.DeviceIdType.MESH


def lookup(values_table, indices):
    matches = indices[..., None] == lax.broadcasted_iota(
        jnp.int32, indices.shape + values_table.shape, indices.ndim
    )
    return jnp.sum(jnp.where(matches, values_table, 0), axis=-1)


def placement(host_expert, owned_experts, devices):
    experts = owned_experts * devices
    matches = host_expert[None, :] == lax.broadcasted_iota(jnp.int32, (experts, devices), 0)
    helper_ids = lax.broadcasted_iota(jnp.int32, (experts, devices), 1)
    helper_of = jnp.sum(jnp.where(matches, helper_ids, 0), axis=1)
    listed = jnp.sum(matches.astype(jnp.int32), axis=1)
    return (helper_of, listed)


def targets(routing, replica, host_expert, owned_experts, devices, slot_rows, groups):
    helper_of, listed = placement(host_expert, owned_experts, devices)
    choices = routing.shape[0] // groups * routing.shape[1]
    usable = (replica == 0) | (lookup(listed, routing) > 0)
    device_to = jnp.where(replica == 0, routing // owned_experts, lookup(helper_of, routing))
    block_to = jnp.where(replica == 0, routing % owned_experts, owned_experts)
    labels = (routing * 2 + replica).reshape(groups, choices)
    earlier = lax.broadcasted_iota(jnp.int32, (choices, choices), 1) < lax.broadcasted_iota(
        jnp.int32, (choices, choices), 0
    )
    matching = (labels[:, :, None] == labels[:, None, :]) & earlier[None]
    ranking = jnp.sum(matching.astype(jnp.int32), axis=2).reshape(routing.shape)
    group_ids = lax.broadcasted_iota(jnp.int32, (groups, choices), 0).reshape(routing.shape)
    position = ((block_to * groups + group_ids) * devices + device_to) * slot_rows + ranking
    return jnp.where(usable, position, -1)


def selector(position, total_slots):
    matches = position[None, :, :] == lax.broadcasted_iota(
        jnp.int32, (total_slots,) + position.shape, 0
    )
    picker = jnp.sum(matches.astype(jnp.float32), axis=2).astype(jnp.bfloat16)
    return (matches, picker)


def fill_rows(matches, picker, tokens, grad_out, gates):
    row_x = jnp.dot(picker, tokens, preferred_element_type=jnp.float32).astype(jnp.bfloat16)
    row_dy = jnp.dot(picker, grad_out, preferred_element_type=jnp.float32).astype(jnp.bfloat16)
    row_gate = jnp.sum(
        jnp.where(matches, gates[None].astype(jnp.float32), 0.0), axis=(1, 2)
    ).astype(jnp.bfloat16)
    return (row_x, row_dy, row_gate)


def expert_block(inputs, upstream, weight, gate_up, down_matrix):
    mixed = jnp.einsum("rd,jfd->jrf", inputs, gate_up, preferred_element_type=jnp.float32)
    gate_pre = mixed[0]
    up_part = mixed[1]
    sigmoid_gate = jax.nn.sigmoid(gate_pre)
    active = gate_pre * sigmoid_gate
    hidden = (active * up_part).astype(jnp.bfloat16)
    output_part = jnp.einsum("rf,fd->rd", hidden, down_matrix, preferred_element_type=jnp.float32)
    gate_part = jnp.sum(output_part * upstream.astype(jnp.float32), axis=1)
    scaled = (weight.astype(jnp.float32)[:, None] * upstream.astype(jnp.float32)).astype(
        jnp.bfloat16
    )
    grad_hidden = jnp.einsum("rd,fd->rf", scaled, down_matrix, preferred_element_type=jnp.float32)
    grad_gate = grad_hidden * up_part * sigmoid_gate * (1.0 + gate_pre * (1.0 - sigmoid_gate))
    grad_mixed = jnp.stack([grad_gate, grad_hidden * active], axis=0).astype(jnp.bfloat16)
    input_part = jnp.einsum("jrf,jfd->rd", grad_mixed, gate_up, preferred_element_type=jnp.float32)
    weight_gu = jnp.einsum("jrf,rd->jfd", grad_mixed, inputs, preferred_element_type=jnp.float32)
    weight_down = jnp.einsum("rf,rd->fd", hidden, scaled, preferred_element_type=jnp.float32)
    return (input_part, gate_part, weight_gu, weight_down)


def shards(tokens, grad_out, routing, replica, gates, host_expert, w_gate_up, w_down):
    devices = lax.axis_size("expert")
    device_id = lax.axis_index("expert")
    token_rows, features = tokens.shape
    owned_experts = w_gate_up.shape[0]
    quarter = w_down.shape[1]
    topk_width = routing.shape[1]
    slot_rows = token_rows * topk_width // (owned_experts * devices)
    blocks = owned_experts + 1
    lane_rows = devices * slot_rows
    piece_rows = quarter // devices
    home_slots = targets(routing, replica, host_expert, owned_experts, devices, slot_rows, 1)
    home_matches, home_picker = selector(home_slots, blocks * lane_rows)
    row_x, row_dy, row_gate = fill_rows(home_matches, home_picker, tokens, grad_out, gates)
    sent_x, sent_dy, sent_gate = (
        lax.all_to_all(
            row_x.reshape(blocks, lane_rows, features),
            "expert",
            split_axis=1,
            concat_axis=1,
            tiled=True,
        ),
        lax.all_to_all(
            row_dy.reshape(blocks, lane_rows, features),
            "expert",
            split_axis=1,
            concat_axis=1,
            tiled=True,
        ),
        lax.all_to_all(
            row_gate.reshape(blocks, lane_rows), "expert", split_axis=1, concat_axis=1, tiled=True
        ),
    )
    block_x, block_dy, block_gate = (
        lax.all_gather(sent_x, "dp", axis=1, tiled=True),
        lax.all_gather(sent_dy, "dp", axis=1, tiled=True),
        lax.all_gather(sent_gate, "dp", axis=1, tiled=True),
    )
    owner_of_helper = host_expert // owned_experts
    owns_copy = owner_of_helper == device_id
    copied_local = jnp.sum(jnp.where(owns_copy, host_expert % owned_experts, 0))
    helper_ids = lax.broadcasted_iota(jnp.int32, (devices, devices), 1)
    owner_ids = lax.broadcasted_iota(jnp.int32, (devices, devices), 0)
    helper_of_owner = jnp.sum(
        jnp.where(owner_of_helper[None, :] == owner_ids, helper_ids, 0), axis=1
    )
    source_gu = lax.dynamic_index_in_dim(w_gate_up, copied_local, 0, keepdims=False)
    source_down = lax.dynamic_index_in_dim(w_down, copied_local, 0, keepdims=False)
    spread_gu, spread_down = (
        lax.all_to_all(
            source_gu.reshape(2, devices, piece_rows, features),
            "expert",
            split_axis=1,
            concat_axis=1,
            tiled=True,
        ),
        lax.all_to_all(
            source_down.reshape(1, devices, piece_rows, features),
            "expert",
            split_axis=1,
            concat_axis=1,
            tiled=True,
        ),
    )
    spread_gu = jnp.take(spread_gu, owner_of_helper, axis=1)
    spread_down = jnp.take(spread_down, owner_of_helper, axis=1)
    hosted_gu, hosted_down = (
        lax.all_to_all(spread_gu, "expert", split_axis=1, concat_axis=1, tiled=True),
        lax.all_to_all(spread_down, "expert", split_axis=1, concat_axis=1, tiled=True),
    )
    hosted_gu = hosted_gu.reshape(2, quarter, features)
    hosted_down = hosted_down.reshape(quarter, features)
    input_parts = []
    gate_parts = []
    owner_gu = []
    owner_down = []
    for block in range(blocks):
        if block < owned_experts:
            gate_up = w_gate_up[block]
            down_matrix = w_down[block]
        else:
            gate_up = hosted_gu
            down_matrix = hosted_down
        input_part, gate_part, weight_gu, weight_down = expert_block(
            block_x[block], block_dy[block], block_gate[block], gate_up, down_matrix
        )
        input_parts.append(input_part.astype(jnp.bfloat16))
        gate_parts.append(gate_part.astype(jnp.bfloat16))
        owner_gu.append(weight_gu)
        owner_down.append(weight_down)
    helper_gu = owner_gu[owned_experts].astype(jnp.bfloat16)
    helper_down = owner_down[owned_experts].astype(jnp.bfloat16)
    back_gu, back_down = (
        lax.all_to_all(
            helper_gu.reshape(2, devices, piece_rows, features),
            "expert",
            split_axis=1,
            concat_axis=1,
            tiled=True,
        ),
        lax.all_to_all(
            helper_down.reshape(1, devices, piece_rows, features),
            "expert",
            split_axis=1,
            concat_axis=1,
            tiled=True,
        ),
    )
    back_gu = jnp.take(back_gu, helper_of_owner, axis=1)
    back_down = jnp.take(back_down, helper_of_owner, axis=1)
    extra_gu, extra_down = (
        lax.all_to_all(back_gu, "expert", split_axis=1, concat_axis=1, tiled=True),
        lax.all_to_all(back_down, "expert", split_axis=1, concat_axis=1, tiled=True),
    )
    extra_gu = extra_gu.reshape(2, quarter, features).astype(jnp.float32)
    extra_down = extra_down.reshape(quarter, features).astype(jnp.float32)
    stacked_dx = jnp.stack(input_parts, axis=0)
    stacked_dg = jnp.stack(gate_parts, axis=0)
    summed_dx, summed_dg = (
        lax.psum_scatter(stacked_dx, "dp", scatter_dimension=1, tiled=True).astype(jnp.float32),
        lax.psum_scatter(stacked_dg, "dp", scatter_dimension=1, tiled=True).astype(jnp.float32),
    )
    row_dx = summed_dx.astype(jnp.bfloat16)
    row_dg = summed_dg.astype(jnp.bfloat16)
    home_dx, home_dg = (
        lax.all_to_all(row_dx, "expert", split_axis=1, concat_axis=1, tiled=True),
        lax.all_to_all(row_dg, "expert", split_axis=1, concat_axis=1, tiled=True),
    )
    home_dx = home_dx.reshape(blocks * lane_rows, features)
    home_dg = home_dg.reshape(blocks * lane_rows).astype(jnp.float32)
    grad_tokens = jnp.einsum(
        "st,sd->td", home_picker, home_dx, preferred_element_type=jnp.float32
    ).astype(jnp.bfloat16)
    grad_gates = jnp.sum(jnp.where(home_matches, home_dg[:, None, None], 0.0), axis=0)
    grad_gu = []
    grad_down = []
    for block in range(owned_experts):
        present = (copied_local == block).astype(jnp.float32)
        grad_gu.append((owner_gu[block] + present * extra_gu).astype(jnp.bfloat16))
        grad_down.append((owner_down[block] + present * extra_down).astype(jnp.bfloat16))
    return (grad_tokens, grad_gates, jnp.stack(grad_gu, axis=0), jnp.stack(grad_down, axis=0))


OWN, ACROSS, ALONG, DIAGONAL = range(4)
PARTNER, TO_X, TO_Y, INNER, OUTER, FAR_MID, FAR_END = range(7)
OWN_X, OWN_Y, OWN_INNER, OWN_OUTER, OWN_FAR_MID, OWN_FAR_END = range(6)
ACROSS_Y, ALONG_X, ACROSS_OUTER, ALONG_OUTER, DIAGONAL_INNER, DIAGONAL_OUTER = range(6, 12)
BOXES = 12
OUTER_BOXES = (OWN_OUTER, ACROSS_OUTER, ALONG_OUTER, DIAGONAL_OUTER)
END, MID = range(2)

GROUPS = (
    ((OWN, 0), (OWN, 1), (ACROSS, 0), (ALONG, 0),),
    ((DIAGONAL, 0), (OWN, 2), (ACROSS, 1), (ALONG, 1),),
    ((OWN, 3), (ACROSS, 2), (ALONG, 2), (DIAGONAL, 2),),
    ((DIAGONAL, 3), (DIAGONAL, 1),),
    ((ACROSS, 3), (ALONG, 3),),
)
ARRIVE, SEND, COMBINE, SUM = range(1, 5)
WHOLE = 2

SCHEDULE = (
    (
        (
            20001, 20020, 20003, 20012, 20013, 20011, 20002, 12010, 11000, 22011,
            21002, 10100, 11010, 20101, 20102, 13000, 10110, 12000, 21020, 20112,
            13010, 10210, 20120, 20111, 23013, 20212, 20211, 22020, 23020, 23003,
            10200, 12100, 20220, 20201,
        ),
        (
            12110, 22120, 20202, 11100, 11110, 21120,
        ),
        (
            22111,
        ),
        (
            10310, 20311, 12210, 21102, 10300, 20302, 30100, 32000, 20312,
        ),
        (
            20301, 20320, 11200, 40110, 31100, 42000, 11210, 12200, 22220, 31000,
            21220, 32100, 13200, 42100, 13210, 23220, 13110, 13100, 41110, 41100,
        ),
        (),
        (
            33000, 23120, 30000, 30300, 11310, 42110, 31200, 13310, 41200, 32200,
            13300, 23320, 42200, 11300, 41010, 21320, 42210, 12300, 30200, 12310,
            33200, 22320, 41210, 43210, 43200,
        ),
        (),
        (
            40200, 33300, 43300, 43310, 33100, 43110,
        ),
        (),
        (
            43100, 40210, 31300, 41300, 32300, 42300, 42310, 41310,
        ),
        (
            43010, 43000, 40300,
        ),
        (
            40310,
        ),
        (
            40100, 42010, 41000,
        ),
        (),
        (
            40000, 40010,
        ),
    ),
    (
        (
            20014, 20001, 20013, 20012, 20020, 20003, 20002, 20004, 20011, 11000,
            10210, 12010, 10100, 22011, 20103, 21002, 20214, 10200, 10110, 12000,
            20112, 20101, 20204, 11010, 20111, 21020, 20113, 20102, 20202, 20201,
            22020, 10300, 20304, 20120, 13000, 13010, 23003,
        ),
        (
            23013, 20220, 20212, 20302, 23020, 10310, 20314, 11100,
        ),
        (
            20211, 11110, 21120, 12100, 12110, 20301, 13110, 13200, 22120, 31000,
            30000, 23113, 20320, 23204,
        ),
        (
            13210, 13100, 23220, 12200, 23103, 23214, 20311,
        ),
        (
            20312, 11210, 11200, 21220, 12210, 30100, 13310, 22220, 31100, 23314,
            32100, 23120, 41110,
        ),
        (
            11300, 13300, 23304, 42110, 41100, 23320,
        ),
        (),
        (
            12310, 12300,
        ),
        (
            31200, 11310, 21320, 32000, 41200, 42100, 30200, 22320, 33300, 43310,
            32200, 33100, 41010, 30300, 43300, 43100,
        ),
        (
            42200,
        ),
        (
            32300, 43110, 42300, 33200, 31300, 43210, 42310, 41300, 40100, 40110,
            43200, 42210, 41310, 40200, 33000, 40300, 43010,
        ),
        (
            41210, 40310, 43000, 42010,
        ),
        (
            42000, 41000, 40210,
        ),
        (),
        (),
        (
            40000, 40010,
        ),
    ),
)


PLACES = sum(GROUPS, ())
SWAPPED = (1, 0, 2, 3)
CROSSED = (2, 3, 0, 1)


def place(role, near):
    return PLACES.index((role, near))


def seen_from(kind, way, role, near):
    if way == TO_X:
        return role ^ 1, near
    if way == TO_Y:
        return role ^ 2, near
    if way == PARTNER:
        return role, near
    if way == FAR_MID or way == FAR_END:
        return role, 3 - near
    return role, (CROSSED if kind == MID and way == INNER else SWAPPED)[near]


def parent(kind, role, near, part):
    if kind == END and near == 1:
        return INNER
    if role == ACROSS:
        return TO_X
    if role == ALONG:
        return TO_Y
    if role == DIAGONAL and (near == 0 or near == 3):
        return (TO_Y, TO_X)[part]
    if near == 0:
        return None
    if near == 3:
        return FAR_END
    return OUTER if near == 1 else INNER


def children(kind, role, near, part):
    if kind == END and near == 1:
        return ()
    fed = kind == MID and (near == 0 or (near == 2 and role in (OWN, DIAGONAL)))
    boxes = (OUTER_BOXES[role],) if fed else ()
    if role == ACROSS or role == ALONG:
        sided = (near == 0 or near == 3) and part == (0 if role == ACROSS else 1)
        return boxes + ((ACROSS_Y if role == ACROSS else ALONG_X,) if sided else ())
    if role == DIAGONAL:
        return boxes + ((DIAGONAL_INNER,) if near == 0 else ())
    boxes += (OWN_X, OWN_Y)
    if near == 0:
        boxes += (OWN_INNER,)
        if kind == END:
            boxes += (OWN_FAR_MID, OWN_FAR_END)
    return boxes


def usable_choices(routing, replica, host_ref):
    usable = replica == 0
    for index in range(host_ref.shape[0]):
        usable = usable | (routing == host_ref[index])
    return usable


def fused_kernel(
    experts,
    tokens_hbm,
    grad_out_hbm,
    routing_hbm,
    replica_hbm,
    gates_hbm,
    host_hbm,
    gu_hbm,
    down_hbm,
    tokens_out,
    gates_out,
    grad_gu_ref,
    grad_down_ref,
    rows_ref,
    gu_ref,
    down_ref,
    gu_turned_ref,
    down_turned_ref,
    mixed_ref,
    hidden_ref,
    part_ref,
    paired_ref,
    inbox_ref,
    gate_sums_ref,
    routing_ref,
    replica_ref,
    gates_ref,
    host_ref,
    local,
    sent,
    landed,
    pair_sent,
    pair_landed,
    sums_sent,
    sums_landed,
):
    dp = lax.axis_index("dp")
    expert = lax.axis_index("expert")
    height, core = expert // 2, expert % 2
    row, column = dp // 2, dp % 2
    depth = rows_ref.shape[0] // 4
    count = rows_ref.shape[2]
    half = count // 2
    features = tokens_hbm.shape[1]
    lanes = rows_ref.shape[3] - 2 * features
    owned, quarter = down_hbm.shape[:2]
    hidden_units = owned * quarter
    across = row * 2 + 1 - column
    along = (1 - row) * 2 + column
    upper = height // (depth // 2)
    outer_level = height + 1 - 2 * (height % 2)
    is_mid = (height + upper) % 2 == 1
    is_end = (height + upper) % 2 == 0
    inner_level = height + 1 - 2 * upper
    targets_of = (
        (dp, height * 2 + 1 - core),
        (across, expert),
        (along, expert),
        (dp, inner_level * 2 + core),
        (dp, outer_level * 2 + core),
        (dp, (depth // 2 - upper) * 2 + core),
        (dp, (depth - 1) * (1 - upper) * 2 + core),
    )
    kinds = [None]
    unsent = ([], [])
    shared = []

    def within(kind, body):
        kinds[0] = kind

        @pl.when(is_end if kind == END else is_mid)
        def _():
            body()

        kinds[0] = None

    def begin(make, *args):
        make(*args).start()
        (shared if kinds[0] is None else unsent[kinds[0]]).append((make, args))

    mine = place(OWN, 0)
    loads = [
        pltpu.make_async_copy(routing_hbm, routing_ref, local.at[0]),
        pltpu.make_async_copy(replica_hbm, replica_ref, local.at[1]),
        pltpu.make_async_copy(gates_hbm, gates_ref, local.at[2]),
        pltpu.make_async_copy(host_hbm, host_ref, local.at[3]),
        pltpu.make_async_copy(tokens_hbm, rows_ref.at[mine, core, :, pl.ds(0, features)], local.at[4]),
        pltpu.make_async_copy(
            grad_out_hbm, rows_ref.at[mine, core, :, pl.ds(features, features)], local.at[5]
        ),
    ]
    for index in range(2 * owned):
        loads.append(
            pltpu.make_async_copy(
                gu_hbm.at[index % owned, index // owned],
                gu_ref.at[pl.ds(index * quarter, quarter)],
                local.at[6 + index],
            )
        )
    for index in range(owned):
        loads.append(
            pltpu.make_async_copy(
                down_hbm.at[index],
                down_ref.at[pl.ds(index * quarter, quarter)],
                local.at[6 + 2 * owned + index],
            )
        )
    for load in loads[:6]:
        load.start()
    barrier = pltpu.get_barrier_semaphore()
    for way in (PARTNER, TO_X, TO_Y, INNER):
        pl.semaphore_signal(barrier, inc=1, device_id=targets_of[way], device_id_type=MESH)

    @pl.when(is_mid)
    def _():
        pl.semaphore_signal(barrier, inc=1, device_id=targets_of[OUTER], device_id_type=MESH)

    for load in loads[:4]:
        load.wait()
    routing = routing_ref[...]
    usable = usable_choices(routing, replica_ref[...], host_ref)
    gates = jnp.where(usable, gates_ref[...].astype(jnp.float32), 0.0)
    weights = jnp.concatenate(
        [
            jnp.sum(jnp.where(routing == index, gates, 0.0), axis=0, keepdims=True)
            for index in range(experts)
        ]
        + [jnp.zeros((lanes - experts, count), jnp.float32)],
        axis=0,
    )
    weights = weights.T
    side = weights[:half] + pltpu.roll(weights[half:], lanes // 2, 1)
    rows_ref[mine, core, :half, 2 * features :] = side.astype(jnp.bfloat16)
    for load in loads[4:6]:
        load.wait()
    pl.semaphore_wait(barrier, 4 + is_mid.astype(jnp.int32))
    for load in loads[6:]:
        load.start()

    def piece(part):
        return pl.ds(part * half, half)

    def span_of(part, width):
        return pl.ds(0, width + lanes if part == 0 else width)

    def row_copy(role, near, part, way):
        at, to = place(role, near), place(*seen_from(kinds[0], way, role, near))
        if part is None:
            span = (slice(None), slice(None))
        else:
            span = (piece(part), span_of(part, 2 * features))
        index = 0 if part is None else part
        return pltpu.make_async_remote_copy(
            src_ref=rows_ref.at[(at, core) + span],
            dst_ref=rows_ref.at[(to, core) + span],
            send_sem=sent.at[at, way * 2 + index],
            recv_sem=landed.at[to, core, index],
            device_id=targets_of[way],
            device_id_type=MESH,
        )

    def partner_rows(role, near):
        at = place(role, near)
        block = rows_ref.at[at, 1 - core]
        pltpu.make_async_remote_copy(
            src_ref=block,
            dst_ref=block,
            send_sem=sent.at[at, 0],
            recv_sem=landed.at[at, 1 - core, 0],
            device_id=targets_of[PARTNER],
            device_id_type=MESH,
        ).wait_recv()

    def rows_by_rows(a, b):
        return jnp.dot(a, b, preferred_element_type=jnp.float32)

    def columns_by_columns(a, b):
        return lax.dot_general(
            a, b, (((0,), (0,)), ((), ())), preferred_element_type=jnp.float32
        ).astype(jnp.bfloat16)

    chip_rows = 2 * count

    def pair_copy(at):
        return pltpu.make_async_remote_copy(
            src_ref=part_ref.at[at, 1 - core],
            dst_ref=paired_ref.at[at],
            send_sem=pair_sent.at[at],
            recv_sem=pair_landed.at[at],
            device_id=targets_of[PARTNER],
            device_id_type=MESH,
        )

    def stacked(ref, index, first, size):
        group = GROUPS[index]
        start = place(*group[0])
        rows = ref[start : start + len(group), ..., first : first + size]
        return rows.reshape(len(group) * chip_rows, size)

    def keep(ref, index, first, values):
        start, stop = place(*GROUPS[index][0]), place(*GROUPS[index][-1]) + 1
        size = values.shape[1]
        shape = (stop - start,) + ref.shape[1:-1] + (size,)
        ref[start:stop, ..., first : first + size] = values.reshape(shape)

    def ahead(group):
        for role, near in GROUPS[group]:
            partner_rows(role, near)
        start, size = place(*GROUPS[group][0]), len(GROUPS[group])
        packed = rows_ref[start : start + size, :, :half, 2 * features :].astype(jnp.float32)
        packed = packed.reshape(2 * size * half, lanes)
        turned = pltpu.roll(packed, lanes // 2, 1)
        side = jnp.concatenate(
            [packed.reshape(2 * size, half, lanes), turned.reshape(2 * size, half, lanes)], axis=1
        ).reshape(2 * size * count, lanes)
        slots = lax.broadcasted_iota(jnp.int32, side.shape, 1)
        shape = (side.shape[0], hidden_units)
        units = lax.broadcasted_iota(jnp.int32, shape, 1)
        at_expert = [slots == expert * owned + index for index in range(owned)]
        of_expert = [
            (units >= index * quarter) & (units < (index + 1) * quarter) for index in range(owned)
        ]
        weight = jnp.zeros(shape, jnp.float32)
        for index in range(owned):
            scale = jnp.sum(jnp.where(at_expert[index], side, 0.0), axis=1, keepdims=True)
            weight = jnp.where(of_expert[index], scale, weight)
        mixed = rows_by_rows(stacked(rows_ref, group, 0, features), gu_turned_ref[...])
        raw_hidden = rows_by_rows(stacked(rows_ref, group, features, features), down_turned_ref[...])
        gate_pre = mixed[:, :hidden_units]
        up_part = mixed[:, hidden_units:]
        sigmoid_gate = jax.nn.sigmoid(gate_pre)
        active = gate_pre * sigmoid_gate
        hidden = (active * up_part).astype(jnp.bfloat16).astype(jnp.float32)
        gate_parts = hidden * raw_hidden
        gate_side = jnp.zeros(side.shape, jnp.float32)
        for index in range(owned):
            total = jnp.sum(
                jnp.where(of_expert[index], gate_parts, 0.0), axis=1, keepdims=True
            )
            gate_side = jnp.where(at_expert[index], total, gate_side)
        grad_hidden = raw_hidden * weight
        grad_gate = (
            grad_hidden * up_part * sigmoid_gate * (1.0 + gate_pre * (1.0 - sigmoid_gate))
        ).astype(jnp.bfloat16)
        grad_up = (grad_hidden * active).astype(jnp.bfloat16)
        weighted = (hidden * weight).astype(jnp.bfloat16)
        gate_side = gate_side.reshape(2 * size, count, lanes)
        low = gate_side[:, :half].reshape(2 * size * half, lanes)
        high = gate_side[:, half:].reshape(2 * size * half, lanes)
        packed = (low + pltpu.roll(high, lanes // 2, 1)).astype(jnp.bfloat16)
        part_ref[start : start + size, :, :half, features:] = packed.reshape(
            size, 2, half, lanes
        )
        keep(hidden_ref, group, 0, weighted)
        keep(mixed_ref, group, 0, grad_gate)
        keep(mixed_ref, group, hidden_units, grad_up)

    def back(group):
        dx = jnp.dot(
            stacked(mixed_ref, group, 0, 2 * hidden_units),
            gu_ref[...],
            preferred_element_type=jnp.float32,
        )
        keep(part_ref, group, 0, dx.astype(jnp.bfloat16))
        for role, near in GROUPS[group]:
            begin(pair_copy, place(role, near))

    def combine(role, near):
        at = place(role, near)
        pair_copy(at).wait_recv()
        for part in range(2):
            span = (piece(part), span_of(part, features))
            part_ref[(at, core) + span] = (
                part_ref[(at, core) + span].astype(jnp.float32)
                + paired_ref[(at,) + span].astype(jnp.float32)
            ).astype(jnp.bfloat16)

    def box_index(box, near, part):
        return (box * depth + near) * 2 + part

    def sum_copy(role, near, part, way, box):
        index = box_index(box, seen_from(kinds[0], way, role, near)[1], part)
        width = span_of(part, features)
        return pltpu.make_async_remote_copy(
            src_ref=part_ref.at[place(role, near), core, piece(part), width],
            dst_ref=inbox_ref.at[index, :, width],
            send_sem=sums_sent.at[box_index(box, near, part)],
            recv_sem=sums_landed.at[index],
            device_id=targets_of[way],
            device_id_type=MESH,
        )

    def incoming(role, near, part, box):
        index = box_index(box, near, part)
        width = span_of(part, features)
        pltpu.make_async_remote_copy(
            src_ref=inbox_ref.at[index, :, width],
            dst_ref=inbox_ref.at[index, :, width],
            send_sem=sums_sent.at[index],
            recv_sem=sums_landed.at[index],
            device_id=targets_of[PARTNER],
            device_id_type=MESH,
        ).wait_recv()
        return inbox_ref[index, :, width].astype(jnp.float32)

    def home_box(role, way):
        if way == TO_X:
            return ALONG_X if role == DIAGONAL else OWN_X
        if way == TO_Y:
            return ACROSS_Y if role == DIAGONAL else OWN_Y
        if way == FAR_END:
            return OWN_FAR_END if kinds[0] == END else OWN_FAR_MID
        if kinds[0] == END:
            return OUTER_BOXES[role]
        return OWN_INNER if role == OWN else DIAGONAL_INNER

    def gather_sums(role, near, part):
        kind = kinds[0]
        at = place(role, near)
        boxes, way = children(kind, role, near, part), parent(kind, role, near, part)
        if boxes:
            span = (piece(part), span_of(part, features))
            value = part_ref[(at, core) + span].astype(jnp.float32)
            for box in boxes:
                value = value + incoming(role, near, part, box)
            if way is None:
                tokens_out[piece(part), :] = value[:, :features].astype(jnp.bfloat16)
                if part == 0:
                    gate_sums_ref[...] = value[:, features:]
            else:
                part_ref[(at, core) + span] = value.astype(jnp.bfloat16)
        if way is not None:
            begin(sum_copy, role, near, part, way, home_box(role, way))

    total_rows = 4 * depth * chip_rows

    def weight_grad(ref, out_ref, source, first, size):
        sources = rows_ref[:, :, :, source * features : (source + 1) * features]
        grads = columns_by_columns(
            ref[:, :, first : first + size].reshape(total_rows, size),
            sources.reshape(total_rows, features),
        )
        start = first
        while start < first + size:
            index, offset = start // quarter, start % quarter
            taken = min(quarter - offset, first + size - start)
            where = (index % owned, index // owned) if source == 0 else (index,)
            out_ref[where + (pl.ds(offset, taken),)] = grads[start - first : start - first + taken]
            start += taken

    jobs = []
    for first in range(0, 2 * hidden_units, 256):
        size = min(256, 2 * hidden_units - first)
        jobs.append((mixed_ref, grad_gu_ref, 0, first, size))
    for first in range(0, hidden_units, 256):
        size = min(256, hidden_units - first)
        jobs.append((hidden_ref, grad_down_ref, 1, first, size))

    def play(codes):
        for code in codes:
            action, role, near, part, way = (code // 10**place_of % 10 for place_of in range(4, -1, -1))
            part = None if part == WHOLE else part
            if action == ARRIVE:
                row_copy(role, near, part, PARTNER).wait_recv()
            elif action == SEND:
                begin(row_copy, role, near, part, way)
            elif action == COMBINE:
                combine(role, near)
            else:
                gather_sums(role, near, part)

    stages = []
    for group in range(len(GROUPS)):
        stages.append((ahead, (group,)))
        stages.append((back, (group,)))
    stages += [(weight_grad, job) for job in jobs]
    def opening(codes):
        return next(index for index, code in enumerate(codes) if code // 10000 == ARRIVE)

    for kind in (END, MID):
        codes = SCHEDULE[kind][0]
        within(kind, functools.partial(play, codes[: opening(codes)]))
    for load in loads[6:]:
        load.wait()
    for ref, turned_ref in ((gu_ref, gu_turned_ref), (down_ref, down_turned_ref)):
        for first in range(0, features, 512):
            turned_ref[first : first + 512, :] = ref[:, first : first + 512].T
    for index, codes in enumerate(zip(*SCHEDULE, strict=True)):
        for kind in (END, MID):
            steps = codes[kind][opening(codes[kind]) :] if index == 0 else codes[kind]
            if steps:
                within(kind, functools.partial(play, steps))
        if index < len(stages):
            stages[index][0](*stages[index][1])
    packed = gate_sums_ref[...]
    sums = jnp.concatenate([packed, pltpu.roll(packed, lanes // 2, 1)], axis=0).T
    picked = jnp.zeros(routing.shape, jnp.float32)
    for index in range(experts):
        picked = jnp.where(routing == index, sums[index : index + 1], picked)
    gates_out[...] = jnp.where(usable, picked, 0.0)

    def settle(sends):
        for make, args in sends:
            make(*args).wait_send()

    settle(shared)
    within(END, lambda: settle(unsent[END]))
    within(MID, lambda: settle(unsent[MID]))


def finish_kernel(*refs):
    count = (len(refs) - 1) // 2
    copies = [
        pltpu.make_async_copy(refs[index], refs[count + index], refs[-1].at[index])
        for index in range(count)
    ]
    for copy in copies:
        copy.start()
    for copy in copies:
        copy.wait()


def fused_layer(tokens, grad_out, routing, replica, gates, host_expert, w_gate_up, w_down):
    count, features = tokens.shape
    owned, quarter = w_down.shape[:2]
    size = lax.axis_size("expert")
    experts = owned * size
    depth = size // 2
    chips = 4 * depth
    lanes = (2 * experts + 127) // 128 * 128
    kind = jnp.bfloat16
    width, sums = 2 * features + lanes, features + lanes
    outside = pl.BlockSpec(memory_space=pltpu.HBM)
    inside = pl.BlockSpec(memory_space=pltpu.VMEM)
    boxes = BOXES * depth * 2
    units = owned * quarter
    turned = (routing.shape[1], count)
    results = (
        ((count, features), kind),
        (turned, jnp.float32),
        (w_gate_up.shape, kind),
        (w_down.shape, kind),
    )
    held = pl.pallas_call(
        functools.partial(fused_kernel, experts),
        out_shape=tuple(pltpu.VMEM(*result) for result in results),
        in_specs=[outside] * 8,
        out_specs=(inside,) * 4,
        scratch_shapes=[
            pltpu.VMEM((chips, 2, count, width), kind),
            pltpu.VMEM((2 * units, features), kind),
            pltpu.VMEM((units, features), kind),
            pltpu.VMEM((features, 2 * units), kind),
            pltpu.VMEM((features, units), kind),
            pltpu.VMEM((chips, 2 * count, 2 * units), kind),
            pltpu.VMEM((chips, 2 * count, units), kind),
            pltpu.VMEM((chips, 2, count, sums), kind),
            pltpu.VMEM((chips, count, sums), kind),
            pltpu.VMEM((boxes, count // 2, sums), kind),
            pltpu.VMEM((count // 2, lanes), jnp.float32),
            pltpu.VMEM(turned, jnp.int32),
            pltpu.VMEM(turned, jnp.int32),
            pltpu.VMEM(turned, kind),
            pltpu.SMEM(host_expert.shape, jnp.int32),
            pltpu.SemaphoreType.DMA((6 + 3 * owned,)),
            pltpu.SemaphoreType.DMA((chips, 14)),
            pltpu.SemaphoreType.DMA((chips, 2, 2)),
            pltpu.SemaphoreType.DMA((chips,)),
            pltpu.SemaphoreType.DMA((chips,)),
            pltpu.SemaphoreType.DMA((boxes,)),
            pltpu.SemaphoreType.DMA((boxes,)),
        ],
        compiler_params=pltpu.CompilerParams(
            collective_id=0, has_side_effects=True, vmem_limit_bytes=44 << 20
        ),
    )(
        *(
            pltpu.with_memory_space_constraint(value, pltpu.HBM)
            for value in (
                tokens, grad_out, routing.T, replica.T, gates.T, host_expert, w_gate_up, w_down
            )
        )
    )
    return pl.pallas_call(
        finish_kernel,
        out_shape=tuple(jax.ShapeDtypeStruct(*result) for result in results),
        in_specs=[inside] * 4,
        out_specs=(outside,) * 4,
        scratch_shapes=[pltpu.SemaphoreType.DMA((4,))],
        compiler_params=pltpu.CompilerParams(vmem_limit_bytes=1 << 20),
    )(*held)


def gathered_shards(
    tokens, grad_out, routing, replica, gates, host_expert, w_gate_up, w_down
):
    grad_tokens, grad_gates, grad_gu, grad_down = fused_layer(
        tokens, grad_out, routing, replica, gates, host_expert, w_gate_up, w_down
    )
    return (grad_tokens, grad_gates.T, grad_gu, grad_down)


def serve(tokens, grad_out, routing, replica, gates, host_expert, w_gate_up, w_down):
    grid = lax.axis_size("dp") == 4 and lax.axis_size("expert") == 8
    visits_all = routing.shape[1] >= lax.axis_size("expert")
    body = gathered_shards if grid and visits_all else shards
    return body(tokens, grad_out, routing, replica, gates, host_expert, w_gate_up, w_down)


def solution(mesh):
    in_specs = (
        P(("dp", "expert"), None),
        P(("dp", "expert"), None),
        P(("dp", "expert"), None),
        P(("dp", "expert"), None),
        P(("dp", "expert"), None),
        P(),
        P("expert", None, "dp", None),
        P("expert", "dp", None),
    )
    out_specs = (
        P(("dp", "expert"), None),
        P(("dp", "expert"), None),
        P("expert", None, "dp", None),
        P("expert", "dp", None),
    )
    return jax.shard_map(serve, mesh=mesh, in_specs=in_specs, out_specs=out_specs, check_vma=False)
```
